256 devices in a mesh: grp: 4 (over z_hi, core), sub: 64 (over y, z_lo, x).
Axes of the slice: x: 4, y: 4, z: 8 (z_hi: 2, z_lo: 4; z = z_hi * 4 + z_lo), core: 2. Of those that a mesh axis runs over, the one named last changes fastest.
Arguments:
- operators: float32 [4, 64, 4, 512, 512], P('grp', 'sub'), may hold values from -1 to 6
- counts: int32 [4, 64], P('grp', 'sub'), may hold values from 1 to 4, as said below
- pair_rows: int32 [4, 64, 4, 256], P('grp', 'sub'), may hold values from -256 to 256, as said below
- gap: float32 [4, 64, 4, 256, 128], P('grp', 'sub'), may hold values from -6 to 6
Outputs:
- multipliers: float32 [4, 64, 4, 256, 128], P('grp', 'sub')
- residual: float32 [4, 64, 4, 256, 128], P('grp', 'sub')
The draws below stay inside these ranges and needn't reach their ends.
Inputs may be any that keep to these rules, and one draw needn't show every extreme that they name: `counts`: each group has at least one owner with 4 subdomains. `pair_rows`: for each group, owner and slot the absolute values are a permutation of 1 to 256.
All inputs are finite; a program needn't handle non-finite values.
Results may differ from the reference program's by a relative error of at most 0.00022.
Values sent between devices are 32-bit elements; how exact they have to be, the bound alone decides.
A program may use at most 64 MiB of HBM per device.

```python
import math
import jax
import jax.numpy as jnp
from jax import lax

M = 512
H = 256
RHS = 128
SLOTS = 4
ITERS = 6
GROUPS = 4
OWNERS = 64


def draw_operators(key, part):
    k_diag, k_noise = jax.random.split(jax.random.fold_in(key, 11))
    shape = (GROUPS, OWNERS, SLOTS, M, M)
    noise = jnp.clip(jax.random.normal(k_noise, shape, jnp.float32), -4.0, 4.0)
    noise = noise * (0.75 / math.sqrt(M))
    symmetric = (noise + jnp.swapaxes(noise, 3, 4)) * (1.0 / math.sqrt(2.0))
    diagonal = jax.random.uniform(k_diag, (GROUPS, OWNERS, SLOTS, M), jnp.float32, 2.0, 5.5)
    identity = jnp.eye(M, dtype=jnp.float32)
    return symmetric * (1.0 - identity) + diagonal[..., None] * identity


def draw_counts(key, part):
    k_first, k_second = jax.random.split(jax.random.fold_in(key, 23))
    levels = jax.random.randint(k_first, (GROUPS, OWNERS), 0, 10)
    tally = 1 + (levels >= 6).astype(jnp.int32) + (levels >= 8).astype(jnp.int32) + (levels >= 9).astype(jnp.int32)
    chosen = jax.random.randint(k_second, (GROUPS,), 0, OWNERS)
    busiest = jnp.arange(OWNERS, dtype=jnp.int32)[None, :] == chosen[:, None]
    return jnp.where(busiest, SLOTS, tally).astype(jnp.int32)


def draw_pair_rows(key, part):
    k_first, k_second = jax.random.split(jax.random.fold_in(key, 37))
    shape = (GROUPS, OWNERS, SLOTS, H)
    scores = jax.random.randint(k_first, shape, 0, 1048576) * H + jnp.arange(H, dtype=jnp.int32)
    ordering = jnp.argsort(scores, axis=-1).astype(jnp.int32)
    flips = 2 * jax.random.randint(k_second, shape, 0, 2) - 1
    return ((ordering + 1) * flips).astype(jnp.int32)


def shard_levels(own_key, shape, cuts, least, largest):
    def one(axis_at, parts):
        steps = jax.random.uniform(jax.random.fold_in(jax.random.fold_in(own_key, 6), axis_at), (parts,), jnp.float32, least / len(cuts), largest / len(cuts))
        return jnp.repeat(jnp.exp(steps), shape[axis_at] // parts).reshape((-1,) + (1,) * (len(shape) - axis_at - 1))

    level = one(*cuts[0])
    for cut in cuts[1:]:
        level = level * one(*cut)
    return level


def gaussian(key, shape, deviation, most, shards=(), held_as=jnp.bfloat16):
    values = jax.random.normal(key, shape, jnp.float32) * deviation
    if len(shards) > 0:
        values = shard_levels(key, shape, shards, -0.22, 0.18) * values
    return jnp.clip(values, min=-most, max=most).astype(held_as)


def setup_inputs(seed: int = 0) -> dict:
    keys = jax.random.split(jax.random.key(seed), 5)
    operators = draw_operators(jax.random.fold_in(keys[4], 71), 0)
    counts = draw_counts(jax.random.fold_in(keys[4], 71), 0)
    pair_rows = draw_pair_rows(jax.random.fold_in(keys[4], 71), 0)
    gap = gaussian(keys[3], (GROUPS, OWNERS, SLOTS, H, RHS), 1.0, 6.0, ((0, 4), (1, 64)), jnp.float32)
    return {"operators": operators, "counts": counts, "pair_rows": pair_rows, "gap": gap}


LOWER = 1.0
UPPER = 14.0


def pick_rows(matrix, picks):
    return matrix[picks]


def place_rows(picks, values):
    return jnp.zeros_like(values).at[picks].set(values)


def reference(operators, counts, pair_rows, gap):
    slot_ids = jnp.arange(SLOTS, dtype=jnp.int32)
    owner_ids = jnp.arange(OWNERS, dtype=jnp.int32)
    occupied = slot_ids[None, None, :] < counts[:, :, None]
    final_slot = slot_ids[None, None, :] == counts[:, :, None] - 1
    exists = occupied & jnp.logical_not((owner_ids[None, :, None] == OWNERS - 1) & final_slot)
    live_mask = occupied.astype(jnp.float32)[..., None, None]
    exist_mask = exists.astype(jnp.float32)[..., None, None]
    top_mask = final_slot[..., None, None]
    top_weight = top_mask.astype(jnp.float32)
    row_index = (jnp.abs(pair_rows) - 1).astype(jnp.int32)
    sign_flip = jnp.sign(pair_rows).astype(jnp.float32)[..., None]
    picker = jax.vmap(jax.vmap(jax.vmap(pick_rows)))
    placer = jax.vmap(jax.vmap(jax.vmap(place_rows)))

    def apply_dual(direction):
        final_block = jnp.sum(direction * top_weight, axis=2)
        from_before = jnp.concatenate([jnp.zeros_like(final_block[:, :1]), final_block[:, :-1]], axis=1)
        previous = jnp.concatenate([from_before[:, :, None], direction[:, :, :-1]], axis=2)
        left_rows = -sign_flip * picker(previous, row_index)
        expanded = jnp.concatenate([left_rows, direction], axis=3) * live_mask
        images = jnp.einsum("gsjmn,gsjnr->gsjmr", operators, expanded, precision=lax.Precision.HIGHEST)
        returned = placer(row_index, -sign_flip * images[:, :, :, :H])
        behind = jnp.concatenate([returned[:, 1:, 0], jnp.zeros_like(returned[:, :1, 0])], axis=1)
        back_next = jnp.concatenate([returned[:, :, 1:], jnp.zeros_like(returned[:, :, :1])], axis=2)
        following = jnp.where(top_mask, behind[:, :, None], back_next)
        return (images[:, :, :, H:] + following) * exist_mask

    centre = (UPPER + LOWER) / 2.0
    radius = (UPPER - LOWER) / 2.0
    spread_ratio = centre / radius
    rho_prev = 1.0 / spread_ratio
    residual = gap * exist_mask
    iterate = jnp.zeros_like(residual)
    direction = residual / centre
    for sweep_num in range(ITERS):
        iterate = iterate + direction
        residual = residual - apply_dual(direction)
        if sweep_num < ITERS - 1:
            rho_next = 1.0 / (2.0 * spread_ratio - rho_prev)
            direction = rho_next * rho_prev * direction + (2.0 * rho_next / radius) * residual
            rho_prev = rho_next
    return iterate, residual
```

```python
import functools

import jax
import jax.numpy as jnp
from jax import lax
from jax.experimental import pallas as pl
from jax.experimental.pallas import tpu as pltpu
from jax.sharding import PartitionSpec as P

M = 512
H = 256
RHS = 128
SLOTS = 4
ITERS = 6
CHUNKS = 2
W = RHS // CHUNKS

LOWER = 1.0
UPPER = 14.0
CENTRE = (UPPER + LOWER) / 2.0
RADIUS = (UPPER - LOWER) / 2.0

F32 = jnp.float32
BF16 = jnp.bfloat16


def coefficients():
    spread = CENTRE / RADIUS
    rho = 1.0 / spread
    keep, add = {}, {}
    for t in range(2, ITERS + 1):
        new = 1.0 / (2.0 * spread - rho)
        keep[t] = new * rho
        add[t] = 2.0 * new / RADIUS
        rho = new
    return keep, add


KEEP, ADD = coefficients()


def chosen(table, t):
    if isinstance(t, int):
        return jnp.float32(table[t])
    value = jnp.float32(table[ITERS])
    for k in range(2, ITERS):
        value = jnp.where(t == k, jnp.float32(table[k]), value)
    return value


def halves(x):
    high = x.astype(BF16)
    low = (x - high.astype(F32)).astype(BF16)
    return high, low


def nn(a, b):
    return jnp.dot(a, b, preferred_element_type=F32)


def nt(a, b):
    return lax.dot_general(a, b, (((1,), (1,)), ((), ())), preferred_element_type=F32)


def kernel(cnt_ref, pairs_ref, ops_hbm, gap_hbm, out_x, out_r,
           ops, gap, w_in, w_p, w_q, vb, vp, vf, rf, xf, gap_out, p_out, q_out, gap_in, p_in, q_in,
           load_sem, gap_sem, g_send, g_recv, p_send, p_recv, q_send, q_recv):
    s = lax.axis_index("sub")
    last_owner = lax.axis_size("sub") - 1
    has_left = s > 0
    has_right = s < last_owner
    c = cnt_ref[0, 0]
    final_slot = jnp.clip(c - 1, 0, SLOTS - 1)

    gap_load = pltpu.make_async_copy(gap_hbm.at[0, 0], gap, gap_sem)
    gap_load.start()
    loads = [pltpu.make_async_copy(ops_hbm.at[0, 0, j], ops.at[j], load_sem.at[j]) for j in range(SLOTS)]
    for load in loads:
        load.start()

    barrier = pltpu.get_barrier_semaphore()

    @pl.when(has_left)
    def _():
        pl.semaphore_signal(barrier, inc=1, device_id={"sub": s - 1}, device_id_type=pl.DeviceIdType.MESH)

    @pl.when(has_right)
    def _():
        pl.semaphore_signal(barrier, inc=1, device_id={"sub": s + 1}, device_id_type=pl.DeviceIdType.MESH)

    @pl.when(jnp.logical_not(has_left))
    def _():
        gap_in[...] = jnp.zeros_like(gap_in)
        p_in[...] = jnp.zeros_like(p_in)

    @pl.when(jnp.logical_not(has_right))
    def _():
        q_in[...] = jnp.zeros_like(q_in)

    def to_right(src, dst, send, recv):
        return pltpu.make_async_remote_copy(
            src_ref=src, dst_ref=dst, send_sem=send, recv_sem=recv,
            device_id={"sub": s + 1}, device_id_type=pl.DeviceIdType.MESH)

    def to_left(src, dst, send, recv):
        return pltpu.make_async_remote_copy(
            src_ref=src, dst_ref=dst, send_sem=send, recv_sem=recv,
            device_id={"sub": s - 1}, device_id_type=pl.DeviceIdType.MESH)

    def gap_copy(h):
        return to_right(gap_out.at[h], gap_in.at[h], g_send.at[h], g_recv.at[h])

    def p_copy(t, h):
        return to_right(p_out.at[t, h], p_in.at[t, h], p_send.at[t, h], p_recv.at[t, h])

    def q_copy(t, h):
        return to_left(q_out.at[t, h], q_in.at[t, h], q_send.at[t, h], q_recv.at[t, h])

    gap_load.wait()
    top = jnp.where(has_right, jnp.transpose(gap[final_slot]), 0.0)
    rf[4] = top
    for h in range(CHUNKS):
        gap_out[h] = top[h * W:(h + 1) * W]

    pl.semaphore_wait(barrier, has_left.astype(jnp.int32) + has_right.astype(jnp.int32))

    @pl.when(has_right)
    def _():
        for h in range(CHUNKS):
            gap_copy(h).start()

    for j in range(SLOTS - 1):
        rf[j + 1] = jnp.where(j < c - 1, jnp.transpose(gap[j]), 0.0)
    for i in range(1, 5):
        first = rf[i] * (1.0 / CENTRE)
        vf[i] = first
        xf[i - 1] = first

    rows = lax.broadcasted_iota(jnp.int32, (H, H), 0)
    columns = lax.broadcasted_iota(jnp.int32, (H, H), 1)
    unit = jnp.where(rows == columns, 1.0, 0.0).astype(BF16)

    def selection(pairs):
        sign = jnp.where(pairs > 0, -1.0, 1.0)
        return jnp.where(rows == jnp.abs(pairs) - 1, sign, 0.0).astype(BF16)

    pairs = [pairs_ref[0, 0, j:j + 1, :] for j in range(SLOTS)]
    for load in loads:
        load.wait()

    def turned(picked, block):
        high, low = halves(block)
        return nt(picked, high).astype(BF16), nt(picked, low).astype(BF16)

    last_pairs = jnp.where(c == 1, pairs[0], jnp.where(c == 2, pairs[1], jnp.where(c == 3, pairs[2], pairs[3])))
    rl_high, rl_low = turned(selection(last_pairs), ops[final_slot, H:, :H])
    rr_high, rr_low = turned(unit, ops[final_slot, H:, H:])
    w_p[0, :H] = rl_high
    w_p[1, :H] = rl_low
    w_p[0, H:] = rr_high
    w_p[1, H:] = rr_low

    for j in range(SLOTS):
        picked = selection(pairs[j])
        high, low = turned(picked, ops[j, :H, :H])
        ll_high = nt(high, picked)
        ll_low = nt(low, picked)
        high, low = halves(ops[j, :H, H:])
        lr_high = nt(unit, nn(picked, high).astype(BF16)).astype(BF16)
        lr_low = nt(unit, nn(picked, low).astype(BF16)).astype(BF16)
        if j == 0:
            w_q[0, :H] = ll_high.astype(BF16)
            w_q[1, :H] = ll_low.astype(BF16)
            w_q[0, H:] = lr_high
            w_q[1, H:] = lr_low
        else:
            rr_high, rr_low = turned(unit, ops[j - 1, H:, H:])
            mid_high, mid_low = halves((rr_high.astype(F32) + ll_high) + (rr_low.astype(F32) + ll_low))
            w_in[j - 1, 0, H:2 * H] = mid_high
            w_in[j - 1, 1, H:2 * H] = mid_low
            w_in[j - 1, 0, 2 * H:] = lr_high
            w_in[j - 1, 1, 2 * H:] = lr_low
        if j < SLOTS - 1:
            rl_high, rl_low = turned(picked, ops[j, H:, :H])
            w_in[j, 0, :H] = rl_high
            w_in[j, 1, :H] = rl_low

    def product(x, w):
        both = nn(x, w[0])
        return (both[:W] + both[W:]) + nn(x[:W], w[1])

    def step(t, h):
        part = slice(h * W, (h + 1) * W)
        first = isinstance(t, int) and t == 1
        final = isinstance(t, int) and t == ITERS
        if first:
            @pl.when(has_left)
            def _():
                gap_copy(h).wait_recv()

            ghost_r = gap_in[h]
            ghost = ghost_r * (1.0 / CENTRE)
            end = vf[4, part]
        else:
            keep, add = chosen(KEEP, t), chosen(ADD, t)

            @pl.when(has_left)
            def _():
                p_copy(t - 1, h).wait_recv()

            ghost_r = rf[0, part] - jnp.where(has_left, p_in[t - 1, h] + q_out[t - 1, h], 0.0)
            ghost = keep * vf[0, part] + add * ghost_r

            @pl.when(has_right)
            def _():
                q_copy(t - 1, h).wait_recv()

            end_r = rf[4, part] - jnp.where(has_right, p_out[t - 1, h] + q_in[t - 1, h], 0.0)
            end = keep * vf[4, part] + add * end_r
            rf[4, part] = end_r
            vf[4, part] = end
            xf[3, part] = xf[3, part] + end
        rf[0, part] = ghost_r
        vf[0, part] = ghost
        inner = [vf[j + 1, part] for j in range(3)]

        blocks = [ghost] + [jnp.where(c == j + 1, end, inner[j]) for j in range(3)] + [end]
        before = jnp.where(c == 1, ghost, jnp.where(c == 2, inner[0], jnp.where(c == 3, inner[1], inner[2])))
        split = [halves(b) for b in blocks]
        for i, (high, low) in enumerate(split):
            vb[h, :W, i * H:(i + 1) * H] = high
            vb[h, W:, i * H:(i + 1) * H] = low
        high, low = halves(before)
        vp[h, :W, :H] = high
        vp[h, W:, :H] = low
        vp[h, :W, H:] = split[4][0]
        vp[h, W:, H:] = split[4][1]

        q_out[t, h] = product(vb[h, :, :2 * H], w_q)

        @pl.when(has_left)
        def _():
            q_copy(t, h).start()

        p_out[t, h] = product(vp[h], w_p)
        if not final:
            @pl.when(has_right)
            def _():
                p_copy(t, h).start()

            keep, add = chosen(KEEP, t + 1), chosen(ADD, t + 1)
        for j in range(3):
            y = product(vb[h, :, j * H:(j + 3) * H], w_in.at[j])
            r = rf[j + 1, part] - jnp.where(j < c - 1, y, 0.0)
            rf[j + 1, part] = r
            if not final:
                v = keep * inner[j] + add * r
                vf[j + 1, part] = v
                xf[j, part] = xf[j, part] + v

    for h in range(CHUNKS):
        step(1, h)

    @pl.loop(2, ITERS)
    def _(t):
        for h in range(CHUNKS):
            step(t, h)

    for h in range(CHUNKS):
        step(ITERS, h)

    def placed(blocks, end, j):
        inner = blocks[j] if j < 3 else jnp.zeros_like(end)
        return jnp.transpose(jnp.where(c - 1 == j, end, jnp.where(j < c - 1, inner, 0.0)))

    for j in range(SLOTS):
        out_x[0, 0, j] = placed([xf[0], xf[1], xf[2]], xf[3], j)

    for h in range(CHUNKS):
        part = slice(h * W, (h + 1) * W)

        @pl.when(has_right)
        def _():
            q_copy(ITERS, h).wait_recv()

        rf[4, part] = rf[4, part] - jnp.where(has_right, p_out[ITERS, h] + q_in[ITERS, h], 0.0)
    for j in range(SLOTS):
        out_r[0, 0, j] = placed([rf[1], rf[2], rf[3]], rf[4], j)

    @pl.when(has_right)
    def _():
        for h in range(CHUNKS):
            gap_copy(h).wait_send()

        @pl.loop(1, ITERS)
        def _(t):
            for h in range(CHUNKS):
                p_copy(t, h).wait_send()

    @pl.when(has_left)
    def _():
        @pl.loop(1, ITERS + 1)
        def _(t):
            for h in range(CHUNKS):
                q_copy(t, h).wait_send()


def shards(operators, counts, pair_rows, gap):
    hbm = pl.BlockSpec(memory_space=pltpu.HBM)
    vmem = pl.BlockSpec(memory_space=pltpu.VMEM)
    steps = ITERS + 1
    dma = pltpu.SemaphoreType.DMA
    message = (steps, CHUNKS, W, H)
    block = jax.ShapeDtypeStruct((1, 1, SLOTS, H, RHS), F32)
    return pl.pallas_call(
        kernel,
        out_shape=(block, block),
        in_specs=[pl.BlockSpec(memory_space=pltpu.SMEM), vmem, hbm, hbm],
        out_specs=(vmem, vmem),
        scratch_shapes=[
            pltpu.VMEM((SLOTS, M, M), F32),
            pltpu.VMEM((SLOTS, H, RHS), F32),
            pltpu.VMEM((3, 2, 3 * H, H), BF16),
            pltpu.VMEM((2, 2 * H, H), BF16),
            pltpu.VMEM((2, 2 * H, H), BF16),
            pltpu.VMEM((CHUNKS, 2 * W, 5 * H), BF16),
            pltpu.VMEM((CHUNKS, 2 * W, 2 * H), BF16),
            pltpu.VMEM((5, RHS, H), F32),
            pltpu.VMEM((5, RHS, H), F32),
            pltpu.VMEM((4, RHS, H), F32),
            pltpu.VMEM((CHUNKS, W, H), F32),
            pltpu.VMEM(message, F32),
            pltpu.VMEM(message, F32),
            pltpu.VMEM((CHUNKS, W, H), F32),
            pltpu.VMEM(message, F32),
            pltpu.VMEM(message, F32),
            dma((SLOTS,)),
            dma,
            dma((CHUNKS,)),
            dma((CHUNKS,)),
            dma((steps, CHUNKS)),
            dma((steps, CHUNKS)),
            dma((steps, CHUNKS)),
            dma((steps, CHUNKS)),
        ],
        compiler_params=pltpu.CompilerParams(
            collective_id=0, has_side_effects=True, vmem_limit_bytes=65_798_144),
        name="feti_chebyshev",
    )(counts, pair_rows, operators, gap)


def solution(mesh):
    return jax.shard_map(
        shards,
        mesh=mesh,
        in_specs=(
            P("grp", "sub", None, None, None),
            P("grp", "sub"),
            P("grp", "sub", None, None),
            P("grp", "sub", None, None, None),
        ),
        out_specs=(P("grp", "sub", None, None, None), P("grp", "sub", None, None, None)),
        check_vma=False,
    )
```

```python
import functools

import jax
import jax.numpy as jnp
from jax import lax
from jax.experimental import pallas as pl
from jax.experimental.pallas import tpu as pltpu
from jax.sharding import PartitionSpec as P

M = 512
H = 256
RHS = 128
SLOTS = 4
ITERS = 6
CHUNKS = 2
W = RHS // CHUNKS
STEPS = (ITERS + 1) * CHUNKS

LOWER = 1.0
UPPER = 14.0
CENTRE = (UPPER + LOWER) / 2.0
RADIUS = (UPPER - LOWER) / 2.0

F32 = jnp.float32
BF16 = jnp.bfloat16


def coefficients():
    spread = CENTRE / RADIUS
    rho = 1.0 / spread
    keep, add = {1: 0.0}, {1: 1.0 / CENTRE}
    for t in range(2, ITERS + 1):
        new = 1.0 / (2.0 * spread - rho)
        keep[t] = new * rho
        add[t] = 2.0 * new / RADIUS
        rho = new
    return keep, add


KEEP, ADD = coefficients()


def chosen(table, t):
    value = jnp.float32(table[ITERS])
    for k in range(1, ITERS):
        value = jnp.where(t == k, jnp.float32(table[k]), value)
    return value


def halves(x):
    high = x.astype(BF16)
    low = (x - high.astype(F32)).astype(BF16)
    return high, low


def nn(a, b):
    return jnp.dot(a, b, preferred_element_type=F32)


def nt(a, b):
    return lax.dot_general(a, b, (((1,), (1,)), ((), ())), preferred_element_type=F32)


def product(x, w):
    both = nn(x, w[0])
    return (both[:W] + both[W:]) + nn(x[:W], w[1])


def kernel(far, cnt_ref, pairs_ref, ops_hbm, gap_hbm, out_x, out_r,
           ops, gap, w_in, w_p, w_ll, w_lr, w_far, vb, vp, v_ghost, r_ghost, v_end, r_end, x_end, v_in, r_in, x_in, own,
           p_out, p_got, q_out, q_got, ll_out, ll_got,
           load_sem, gap_sem, ll_sem, p_send, p_recv, q_send, q_recv):
    s = lax.axis_index("sub")
    has_left = s > 0
    has_right = s < lax.axis_size("sub") - 1
    c = cnt_ref[0, 0]
    final_slot = jnp.clip(c - 1, 0, SLOTS - 1)

    gap_load = pltpu.make_async_copy(gap_hbm.at[0, 0], gap, gap_sem)
    gap_load.start()
    loads = [pltpu.make_async_copy(ops_hbm.at[0, 0, j], ops.at[j], load_sem.at[j]) for j in range(SLOTS)]
    for load in loads:
        load.start()

    barrier = pltpu.get_barrier_semaphore()

    @pl.when(has_left)
    def _():
        pl.semaphore_signal(barrier, inc=1, device_id={"sub": s - 1}, device_id_type=pl.DeviceIdType.MESH)

    @pl.when(has_right)
    def _():
        pl.semaphore_signal(barrier, inc=1, device_id={"sub": s + 1}, device_id_type=pl.DeviceIdType.MESH)

    @pl.when(jnp.logical_not(has_left))
    def _():
        p_got[...] = jnp.zeros_like(p_got)

    @pl.when(jnp.logical_not(has_right))
    def _():
        q_got[...] = jnp.zeros_like(q_got)

    for ref in (v_ghost, r_ghost, v_end, r_end, x_end, own, x_in, vp, w_far):
        ref[...] = jnp.zeros_like(ref)
    q_out[0] = jnp.zeros(q_out.shape[1:], F32)
    q_got[0] = jnp.zeros(q_got.shape[1:], F32)

    def p_copy(t, h):
        return pltpu.make_async_remote_copy(
            src_ref=p_out.at[t, h], dst_ref=p_got.at[t, h], send_sem=p_send.at[h], recv_sem=p_recv.at[t, h],
            device_id={"sub": s + 1}, device_id_type=pl.DeviceIdType.MESH)

    def q_copy(t, h):
        return pltpu.make_async_remote_copy(
            src_ref=q_out.at[t, h], dst_ref=q_got.at[t, h], send_sem=q_send.at[h], recv_sem=q_recv.at[t, h],
            device_id={"sub": s - 1}, device_id_type=pl.DeviceIdType.MESH)

    ll_copy = pltpu.make_async_remote_copy(
        src_ref=ll_out, dst_ref=ll_got, send_sem=ll_sem.at[0], recv_sem=ll_sem.at[1],
        device_id={"sub": s - 1}, device_id_type=pl.DeviceIdType.MESH)

    gap_load.wait()
    top = jnp.where(has_right, jnp.transpose(gap[final_slot]), 0.0)
    for h in range(CHUNKS):
        p_out[0, h] = -top[h * W:(h + 1) * W]
    for j in range(SLOTS - 1):
        turned_gap = jnp.where(j < c - 1, jnp.transpose(gap[j]), 0.0)
        for h in range(CHUNKS):
            r = turned_gap[h * W:(h + 1) * W]
            r_in[h, j] = r
            v_in[h, j] = r * (1.0 / CENTRE)

    rows = lax.broadcasted_iota(jnp.int32, (H, H), 0)
    columns = lax.broadcasted_iota(jnp.int32, (H, H), 1)
    unit = jnp.where(rows == columns, 1.0, 0.0).astype(BF16)

    def selection(pairs):
        sign = jnp.where(pairs > 0, -1.0, 1.0)
        return jnp.where(rows == jnp.abs(pairs) - 1, sign, 0.0).astype(BF16)

    def turned(picked, block):
        high, low = halves(block)
        return nt(picked, high).astype(BF16), nt(picked, low).astype(BF16)

    def left_left(picked, j):
        high, low = turned(picked, ops[j, :H, :H])
        return nt(high, picked), nt(low, picked)

    def left_right(picked, j):
        high, low = halves(ops[j, :H, H:])
        return (nt(unit, nn(picked, high).astype(BF16)).astype(BF16),
                nt(unit, nn(picked, low).astype(BF16)).astype(BF16))

    pairs = [pairs_ref[0, 0, j:j + 1, :] for j in range(SLOTS)]
    loads[0].wait()
    picked = selection(pairs[0])
    ll_high, ll_low = left_left(picked, 0)
    ll_out[...] = ll_high + ll_low
    w_ll[0] = ll_high.astype(BF16)
    w_ll[1] = ll_low.astype(BF16)
    w_lr[0], w_lr[1] = left_right(picked, 0)

    for load in loads[1:]:
        load.wait()
    last_pairs = jnp.where(c == 1, pairs[0], jnp.where(c == 2, pairs[1], jnp.where(c == 3, pairs[2], pairs[3])))
    w_p[0, :H], w_p[1, :H] = turned(selection(last_pairs), ops[final_slot, H:, :H])
    w_p[0, H:], w_p[1, H:] = turned(unit, ops[final_slot, H:, H:])

    pl.semaphore_wait(barrier, has_left.astype(jnp.int32) + has_right.astype(jnp.int32))

    @pl.when(has_right)
    def _():
        for h in range(CHUNKS):
            p_copy(0, h).start()

    @pl.when(has_left)
    def _():
        ll_copy.start()

    def end_step(n):
        t, h = n // CHUNKS + 1, n % CHUNKS
        keep, add = chosen(KEEP, t), chosen(ADD, t)

        @pl.when(jnp.logical_and(has_right, n == CHUNKS))
        def _():
            ll_copy.wait_recv()
            w_far[0], w_far[1] = halves(ll_got[...])

        partial = p_out[t - 1, h] + product(vp[h, :, H:], w_far)

        @pl.when(jnp.logical_and(has_right, t > 1))
        def _():
            q_copy(t - 1, h).wait_recv()

        r = r_end[h] - jnp.where(has_right, partial + q_got[t - 1, h], 0.0)
        r_end[h] = r

        @pl.when(t <= ITERS)
        def _():
            end = keep * v_end[h] + add * r
            v_end[h] = end
            x_end[h] = x_end[h] + end
            high, low = halves(end)
            vp[h, :W, H:] = high
            vp[h, W:, H:] = low
            high, low = halves(jnp.where(c == 1, end, v_in[h, 0]))
            vb[h, :W, H:2 * H] = high
            vb[h, W:, H:2 * H] = low

            @pl.when(jnp.logical_and(has_left, t > 1))
            def _():
                q_copy(t - 1, h).wait_send()

            q_out[t, h] = product(vb[h, :, H:2 * H], w_lr)

            @pl.when(has_left)
            def _():
                q_copy(t, h).start()

    def ghost_step(n):
        t, h = n // CHUNKS + 1, n % CHUNKS
        keep, add = chosen(KEEP, t), chosen(ADD, t)
        keep_next, add_next = chosen(KEEP, t + 1), chosen(ADD, t + 1)
        partial = q_out[t - 1, h] + own[h]

        @pl.when(has_left)
        def _():
            p_copy(t - 1, h).wait_recv()

        r = r_ghost[h] - jnp.where(has_left, partial + p_got[t - 1, h], 0.0)
        ghost = keep * v_ghost[h] + add * r
        r_ghost[h] = r
        v_ghost[h] = ghost
        inner = [v_in[h, j] for j in range(3)]
        end = v_end[h]
        before = jnp.where(c == 1, ghost, jnp.where(c == 2, inner[0], jnp.where(c == 3, inner[1], inner[2])))
        high, low = halves(before)
        vp[h, :W, :H] = high
        vp[h, W:, :H] = low
        blocks = {0: ghost, 2: jnp.where(c == 2, end, inner[1]), 3: jnp.where(c == 3, end, inner[2]), 4: end}
        for i, block in blocks.items():
            high, low = halves(block)
            vb[h, :W, i * H:(i + 1) * H] = high
            vb[h, W:, i * H:(i + 1) * H] = low

        @pl.when(has_right)
        def _():
            p_copy(t - 1, h).wait_send()

        p_out[t, h] = product(vp[h], w_p)

        @pl.when(jnp.logical_and(has_right, t < ITERS))
        def _():
            p_copy(t, h).start()

        for j in range(3):
            y = product(vb[h, :, j * H:(j + 3) * H], w_in.at[j])
            r = r_in[h, j] - jnp.where(j < c - 1, y, 0.0)
            r_in[h, j] = r
            x_in[h, j] = x_in[h, j] + inner[j]
            v_in[h, j] = keep_next * inner[j] + add_next * r
        own[h] = product(vb[h, :, :H], w_ll)

    ahead = jnp.where(s % far == 0, CHUNKS, 1)

    @pl.loop(0, ahead)
    def _(n):
        end_step(n)

    for j in range(SLOTS):
        picked = selection(pairs[j])
        if j > 0:
            ll_high, ll_low = left_left(picked, j)
            rr_high, rr_low = turned(unit, ops[j - 1, H:, H:])
            mid_high, mid_low = halves((rr_high.astype(F32) + ll_high) + (rr_low.astype(F32) + ll_low))
            w_in[j - 1, 0, H:2 * H] = mid_high
            w_in[j - 1, 1, H:2 * H] = mid_low
            w_in[j - 1, 0, 2 * H:], w_in[j - 1, 1, 2 * H:] = left_right(picked, j)
        if j < SLOTS - 1:
            w_in[j, 0, :H], w_in[j, 1, :H] = turned(picked, ops[j, H:, :H])

    def placed(inner, end, j):
        kept = jnp.where(j < c - 1, inner, 0.0) if j < 3 else jnp.zeros_like(end)
        return jnp.transpose(jnp.where(c - 1 == j, end, kept))

    @pl.loop(0, ITERS * CHUNKS)
    def _(n):
        ghost_step(n)

        @pl.when(n == ITERS * CHUNKS - 1)
        def _():
            end = x_end[...].reshape(RHS, H)
            for j in range(SLOTS):
                out_x[0, 0, j] = placed(x_in[:, j % 3].reshape(RHS, H), end, j)
                out_r[0, 0, j] = placed(r_in[:, j % 3].reshape(RHS, H), jnp.zeros_like(end), j)

        end_step(n + ahead)

    @pl.loop(ITERS * CHUNKS + ahead, STEPS)
    def _(n):
        end_step(n)

    end = jnp.transpose(r_end[...].reshape(RHS, H))
    for j in range(SLOTS):
        out_r[0, 0, j] = jnp.where(c - 1 == j, end, out_r[0, 0, j])

    @pl.when(has_left)
    def _():
        ll_copy.wait_send()
        for h in range(CHUNKS):
            q_copy(ITERS, h).wait_send()


def shards(far, operators, counts, pair_rows, gap):
    hbm = pl.BlockSpec(memory_space=pltpu.HBM)
    vmem = pl.BlockSpec(memory_space=pltpu.VMEM)
    dma = pltpu.SemaphoreType.DMA
    message = pltpu.VMEM((ITERS + 1, CHUNKS, W, H), F32)
    chunk = pltpu.VMEM((CHUNKS, W, H), F32)
    inner = pltpu.VMEM((CHUNKS, 3, W, H), F32)
    operator = pltpu.VMEM((2, H, H), BF16)
    block = jax.ShapeDtypeStruct((1, 1, SLOTS, H, RHS), F32)
    return pl.pallas_call(
        functools.partial(kernel, far),
        out_shape=(block, block),
        in_specs=[pl.BlockSpec(memory_space=pltpu.SMEM), vmem, hbm, hbm],
        out_specs=(vmem, vmem),
        scratch_shapes=[
            pltpu.VMEM((SLOTS, M, M), F32),
            pltpu.VMEM((SLOTS, H, RHS), F32),
            pltpu.VMEM((3, 2, 3 * H, H), BF16),
            pltpu.VMEM((2, 2 * H, H), BF16),
            operator,
            operator,
            operator,
            pltpu.VMEM((CHUNKS, 2 * W, 5 * H), BF16),
            pltpu.VMEM((CHUNKS, 2 * W, 2 * H), BF16),
            chunk, chunk, chunk, chunk, chunk,
            inner, inner, inner,
            chunk,
            message, message, message, message,
            pltpu.VMEM((H, H), F32),
            pltpu.VMEM((H, H), F32),
            dma((SLOTS,)),
            dma,
            dma((2,)),
            dma((CHUNKS,)),
            dma((ITERS + 1, CHUNKS)),
            dma((CHUNKS,)),
            dma((ITERS + 1, CHUNKS)),
        ],
        compiler_params=pltpu.CompilerParams(
            collective_id=0, has_side_effects=True, vmem_limit_bytes=65_798_144),
        name="feti_chebyshev",
    )(counts, pair_rows, operators, gap)


def solution(mesh):
    return jax.shard_map(
        functools.partial(shards, 16 if mesh.shape["sub"] % 16 == 0 else 2),
        mesh=mesh,
        in_specs=(
            P("grp", "sub", None, None, None),
            P("grp", "sub"),
            P("grp", "sub", None, None),
            P("grp", "sub", None, None, None),
        ),
        out_specs=(P("grp", "sub", None, None, None), P("grp", "sub", None, None, None)),
        check_vma=False,
    )
```

```python
import functools

import jax
import jax.numpy as jnp
from jax import lax
from jax.experimental import pallas as pl
from jax.experimental.pallas import tpu as pltpu
from jax.sharding import PartitionSpec as P

M = 512
H = 256
RHS = 128
SLOTS = 4
ITERS = 6
CHUNKS = 2
W = RHS // CHUNKS

LOWER = 1.0
UPPER = 14.0
CENTRE = (UPPER + LOWER) / 2.0
RADIUS = (UPPER - LOWER) / 2.0

F32 = jnp.float32
BF16 = jnp.bfloat16


def coefficients():
    spread = CENTRE / RADIUS
    rho = 1.0 / spread
    keep, add = {1: 0.0}, {1: 1.0 / CENTRE}
    for t in range(2, ITERS + 1):
        new = 1.0 / (2.0 * spread - rho)
        keep[t] = new * rho
        add[t] = 2.0 * new / RADIUS
        rho = new
    return keep, add


KEEP, ADD = coefficients()


def chosen(table, t):
    value = jnp.float32(table[ITERS])
    for k in range(1, ITERS):
        value = jnp.where(t == k, jnp.float32(table[k]), value)
    return value


def halves(x):
    high = x.astype(BF16)
    low = (x - high.astype(F32)).astype(BF16)
    return high, low


def nn(a, b):
    return jnp.dot(a, b, preferred_element_type=F32)


def nt(a, b):
    return lax.dot_general(a, b, (((1,), (1,)), ((), ())), preferred_element_type=F32)


def kernel(far, cnt_ref, pairs_ref, ops_hbm, gap, out_x, out_r,
           ops, w_in, w_p, w_ll, w_lr, w_far, vb, far_out, v_ghost, r_ghost, v_end, r_end, x_end, v_in, r_in, x_in, own,
           p_out, p_got, q_out, q_got, ll_out, ll_got,
           load_sem, ll_sem, p_send, p_recv, q_send, q_recv):
    s = lax.axis_index("sub")
    has_left = s > 0
    has_right = s < lax.axis_size("sub") - 1
    c = cnt_ref[0, 0]
    final_slot = jnp.clip(c - 1, 0, SLOTS - 1)

    loads = [pltpu.make_async_copy(ops_hbm.at[0, 0, j], ops.at[j], load_sem.at[j]) for j in range(SLOTS)]
    for load in loads:
        load.start()

    barrier = pltpu.get_barrier_semaphore()

    @pl.when(has_left)
    def _():
        pl.semaphore_signal(barrier, inc=1, device_id={"sub": s - 1}, device_id_type=pl.DeviceIdType.MESH)

    @pl.when(has_right)
    def _():
        pl.semaphore_signal(barrier, inc=1, device_id={"sub": s + 1}, device_id_type=pl.DeviceIdType.MESH)

    @pl.when(jnp.logical_not(has_left))
    def _():
        p_got[...] = jnp.zeros_like(p_got)

    @pl.when(jnp.logical_not(has_right))
    def _():
        q_got[...] = jnp.zeros_like(q_got)

    for ref in (v_ghost, r_ghost, v_end, r_end, x_end, own, x_in, far_out, w_far):
        ref[...] = jnp.zeros_like(ref)
    q_out[0] = jnp.zeros(q_out.shape[1:], F32)
    q_got[0] = jnp.zeros(q_got.shape[1:], F32)

    def p_copy(t, h):
        return pltpu.make_async_remote_copy(
            src_ref=p_out.at[t, h], dst_ref=p_got.at[t, h], send_sem=p_send.at[h], recv_sem=p_recv.at[t, h],
            device_id={"sub": s + 1}, device_id_type=pl.DeviceIdType.MESH)

    def q_copy(t, h):
        return pltpu.make_async_remote_copy(
            src_ref=q_out.at[t, h], dst_ref=q_got.at[t, h], send_sem=q_send.at[h], recv_sem=q_recv.at[t, h],
            device_id={"sub": s - 1}, device_id_type=pl.DeviceIdType.MESH)

    ll_copy = pltpu.make_async_remote_copy(
        src_ref=ll_out, dst_ref=ll_got, send_sem=ll_sem.at[0], recv_sem=ll_sem.at[1],
        device_id={"sub": s - 1}, device_id_type=pl.DeviceIdType.MESH)

    top = jnp.where(has_right, jnp.transpose(gap[0, 0, final_slot]), 0.0)
    for h in range(CHUNKS):
        p_out[0, h] = -top[h * W:(h + 1) * W]
    for j in range(SLOTS - 1):
        turned_gap = jnp.where(j < c - 1, jnp.transpose(gap[0, 0, j]), 0.0)
        for h in range(CHUNKS):
            r = turned_gap[h * W:(h + 1) * W]
            r_in[h, j] = r
            v_in[h, j] = r * (1.0 / CENTRE)

    rows = lax.broadcasted_iota(jnp.int32, (H, H), 0)

    def selection(pairs):
        sign = jnp.where(pairs > 0, -1.0, 1.0)
        return jnp.where(rows == jnp.abs(pairs) - 1, sign, 0.0).astype(BF16)

    def turned(picked, block):
        high, low = halves(block)
        return nt(picked, high).astype(BF16), nt(picked, low).astype(BF16)

    def left_left(picked, j):
        high, low = turned(picked, ops[j, :H, :H])
        return nt(high, picked), nt(low, picked)

    def left_right(picked, j):
        high, low = halves(jnp.transpose(ops[j, :H, H:]))
        return nt(high, picked).astype(BF16), nt(low, picked).astype(BF16)

    pairs = [pairs_ref[0, 0, j:j + 1, :] for j in range(SLOTS)]
    loads[0].wait()
    picked = selection(pairs[0])
    ll_high, ll_low = left_left(picked, 0)
    ll_out[...] = ll_high + ll_low
    w_ll[0] = ll_high.astype(BF16)
    w_ll[1] = ll_low.astype(BF16)
    w_lr[0], w_lr[1] = left_right(picked, 0)

    for load in loads[1:]:
        load.wait()
    last_pairs = jnp.where(c == 1, pairs[0], jnp.where(c == 2, pairs[1], jnp.where(c == 3, pairs[2], pairs[3])))
    w_p[0, :H], w_p[1, :H] = turned(selection(last_pairs), ops[final_slot, H:, :H])
    w_p[0, H:], w_p[1, H:] = halves(jnp.transpose(ops[final_slot, H:, H:]))

    pl.semaphore_wait(barrier, has_left.astype(jnp.int32) + has_right.astype(jnp.int32))

    @pl.when(has_right)
    def _():
        for h in range(CHUNKS):
            p_copy(0, h).start()

    @pl.when(has_left)
    def _():
        ll_copy.start()

    def product(x, w):
        high, low = x
        both = nn(jnp.concatenate([high, low], axis=0), w[0])
        return (both[:W] + both[W:]) + nn(high, w[1])

    def end_step(t, h, last):
        keep, add = chosen(KEEP, t), chosen(ADD, t)
        partial = p_out[t - 1, h] + far_out[h]

        @pl.when(jnp.logical_and(has_right, t > 1))
        def _():
            q_copy(t - 1, h).wait_recv()

        r = r_end[h] - jnp.where(has_right, partial + q_got[t - 1, h], 0.0)
        r_end[h] = r

        def rest():
            end = keep * v_end[h] + add * r
            q_out[t, h] = product(halves(jnp.where(c == 1, end, v_in[h, 0])), w_lr)

            @pl.when(has_left)
            def _():
                @pl.when(t > 1)
                def _():
                    q_copy(t - 1, h).wait_send()

                q_copy(t, h).start()

            v_end[h] = end
            x_end[h] = x_end[h] + end
            far_out[h] = product(halves(end), w_far)

        if last:
            pl.when(t <= ITERS)(rest)
        else:
            rest()

    def late_far():
        @pl.when(has_right)
        def _():
            ll_copy.wait_recv()
            w_far[0], w_far[1] = halves(ll_got[...])
            for h in range(CHUNKS):
                far_out[h] = product(halves(v_end[h]), w_far)

    def row(t, h, j):
        y = product((vb[h, :W, j * H:(j + 3) * H], vb[h, W:, j * H:(j + 3) * H]), w_in.at[j])
        r = r_in[h, j] - jnp.where(j < c - 1, y, 0.0)
        v = v_in[h, j]
        r_in[h, j] = r
        x_in[h, j] = x_in[h, j] + v
        v_in[h, j] = chosen(KEEP, t + 1) * v + chosen(ADD, t + 1) * r

    def ghost_step(t, h):
        keep, add = chosen(KEEP, t), chosen(ADD, t)
        partial = q_out[t - 1, h] + own[h]
        inner = [v_in[h, j] for j in range(3)]
        end = v_end[h]

        @pl.when(has_left)
        def _():
            p_copy(t - 1, h).wait_recv()

        r = r_ghost[h] - jnp.where(has_left, partial + p_got[t - 1, h], 0.0)
        ghost = keep * v_ghost[h] + add * r
        before = jnp.where(c == 1, ghost, jnp.where(c == 2, inner[0], jnp.where(c == 3, inner[1], inner[2])))
        end_high, end_low = halves(end)
        high, low = halves(before)
        p_out[t, h] = product((jnp.concatenate([high, end_high], axis=1), jnp.concatenate([low, end_low], axis=1)), w_p)

        @pl.when(has_right)
        def _():
            p_copy(t - 1, h).wait_send()

            @pl.when(t < ITERS)
            def _():
                p_copy(t, h).start()

        r_ghost[h] = r
        v_ghost[h] = ghost
        for i, block in enumerate([ghost] + [jnp.where(c == j + 1, end, inner[j]) for j in range(3)] + [end]):
            high, low = halves(block)
            vb[h, :W, i * H:(i + 1) * H] = high
            vb[h, W:, i * H:(i + 1) * H] = low
        row(t, h, 0)

    def inner_step(t, h):
        row(t, h, 1)
        row(t, h, 2)
        own[h] = product((vb[h, :W, :H], vb[h, W:, :H]), w_ll)

    left_is_far = s % far == 0

    @pl.when(left_is_far)
    def _():
        @pl.loop(0, CHUNKS)
        def _(h):
            end_step(1, h, False)

    for j in range(SLOTS):
        picked = selection(pairs[j])
        if j > 0:
            ll_high, ll_low = left_left(picked, j)
            mid_high, mid_low = halves(jnp.transpose(ops[j - 1, H:, H:]) + (ll_high + ll_low))
            w_in[j - 1, 0, H:2 * H] = mid_high
            w_in[j - 1, 1, H:2 * H] = mid_low
            w_in[j - 1, 0, 2 * H:], w_in[j - 1, 1, 2 * H:] = left_right(picked, j)
        if j < SLOTS - 1:
            w_in[j, 0, :H], w_in[j, 1, :H] = turned(picked, ops[j, H:, :H])

    def placed(inner, end, j):
        kept = jnp.where(j < c - 1, inner, 0.0) if j < 3 else jnp.zeros_like(end)
        return jnp.transpose(jnp.where(c - 1 == j, end, kept))

    @pl.when(left_is_far)
    def _():
        late_far()

        @pl.loop(0, ITERS * CHUNKS)
        def _(n):
            t, h = n // CHUNKS + 1, n % CHUNKS
            ghost_step(t, h)
            end_step(t + 1, h, True)
            inner_step(t, h)

    @pl.when(jnp.logical_not(left_is_far))
    def _():
        @pl.loop(0, ITERS * CHUNKS)
        def _(n):
            t, h = n // CHUNKS + 1, n % CHUNKS
            end_step(t, h, False)
            ghost_step(t, h)
            inner_step(t, h)
            pl.when(n == CHUNKS - 1)(late_far)

    end = x_end[...].reshape(RHS, H)
    for j in range(SLOTS):
        out_x[0, 0, j] = placed(x_in[:, j % 3].reshape(RHS, H), end, j)
        out_r[0, 0, j] = placed(r_in[:, j % 3].reshape(RHS, H), jnp.zeros_like(end), j)

    @pl.when(jnp.logical_and(jnp.logical_not(left_is_far), has_right))
    def _():
        @pl.loop(0, CHUNKS)
        def _(h):
            q_copy(ITERS, h).wait_recv()
            r_end[h] = r_end[h] - (p_out[ITERS, h] + far_out[h] + q_got[ITERS, h])

    end = jnp.transpose(r_end[...].reshape(RHS, H))
    for j in range(SLOTS):
        out_r[0, 0, j] = jnp.where(c - 1 == j, end, out_r[0, 0, j])

    @pl.when(has_left)
    def _():
        ll_copy.wait_send()
        for h in range(CHUNKS):
            q_copy(ITERS, h).wait_send()


def shards(far, operators, counts, pair_rows, gap):
    hbm = pl.BlockSpec(memory_space=pltpu.HBM)
    vmem = pl.BlockSpec(memory_space=pltpu.VMEM)
    dma = pltpu.SemaphoreType.DMA
    message = pltpu.VMEM((ITERS + 1, CHUNKS, W, H), F32)
    chunk = pltpu.VMEM((CHUNKS, W, H), F32)
    inner = pltpu.VMEM((CHUNKS, 3, W, H), F32)
    operator = pltpu.VMEM((2, H, H), BF16)
    block = jax.ShapeDtypeStruct((1, 1, SLOTS, H, RHS), F32)
    return pl.pallas_call(
        functools.partial(kernel, far),
        out_shape=(block, block),
        in_specs=[pl.BlockSpec(memory_space=pltpu.SMEM), vmem, hbm, vmem],
        out_specs=(vmem, vmem),
        scratch_shapes=[
            pltpu.VMEM((SLOTS, M, M), F32),
            pltpu.VMEM((3, 2, 3 * H, H), BF16),
            pltpu.VMEM((2, 2 * H, H), BF16),
            operator,
            operator,
            operator,
            pltpu.VMEM((CHUNKS, 2 * W, 5 * H), BF16),
            chunk, chunk, chunk, chunk, chunk, chunk,
            inner, inner, inner,
            chunk,
            message, message, message, message,
            pltpu.VMEM((H, H), F32),
            pltpu.VMEM((H, H), F32),
            dma((SLOTS,)),
            dma((2,)),
            dma((CHUNKS,)),
            dma((ITERS + 1, CHUNKS)),
            dma((CHUNKS,)),
            dma((ITERS + 1, CHUNKS)),
        ],
        compiler_params=pltpu.CompilerParams(
            collective_id=0, has_side_effects=True, vmem_limit_bytes=54_000_000),
        name="feti_chebyshev",
    )(counts, pair_rows, operators, gap)


def solution(mesh):
    return jax.shard_map(
        functools.partial(shards, 16 if mesh.shape["sub"] % 16 == 0 else 2),
        mesh=mesh,
        in_specs=(
            P("grp", "sub", None, None, None),
            P("grp", "sub"),
            P("grp", "sub", None, None),
            P("grp", "sub", None, None, None),
        ),
        out_specs=(P("grp", "sub", None, None, None), P("grp", "sub", None, None, None)),
        check_vma=False,
    )
```

```python
import functools

import jax
import jax.numpy as jnp
from jax import lax
from jax.experimental import pallas as pl
from jax.experimental.pallas import tpu as pltpu
from jax.sharding import PartitionSpec as P

M = 512
H = 256
RHS = 128
SLOTS = 4
ITERS = 6
CHUNKS = 2
W = RHS // CHUNKS

LOWER = 1.0
UPPER = 14.0
CENTRE = (UPPER + LOWER) / 2.0
RADIUS = (UPPER - LOWER) / 2.0

F32 = jnp.float32
BF16 = jnp.bfloat16


def coefficients():
    spread = CENTRE / RADIUS
    rho = 1.0 / spread
    keep, add = {1: 0.0}, {1: 1.0 / CENTRE}
    for t in range(2, ITERS + 1):
        new = 1.0 / (2.0 * spread - rho)
        keep[t] = new * rho
        add[t] = 2.0 * new / RADIUS
        rho = new
    keep[ITERS + 1] = add[ITERS + 1] = 0.0
    return keep, add


KEEP, ADD = coefficients()


def chosen(table, t):
    value = jnp.float32(table[ITERS + 1])
    for k in range(1, ITERS + 1):
        value = jnp.where(t == k, jnp.float32(table[k]), value)
    return value


def halves(x):
    high = x.astype(BF16)
    low = (x - high.astype(F32)).astype(BF16)
    return high, low


def nn(a, b):
    return jnp.dot(a, b, preferred_element_type=F32)


def nt(a, b):
    return lax.dot_general(a, b, (((1,), (1,)), ((), ())), preferred_element_type=F32)


def kernel(far, cnt_ref, pairs_hbm, ops_hbm, gap_hbm, out_x, out_r,
           ops, gap, pairs_ref, w_in, w_p, w_ll, w_lr, w_far, vb, far_out, v_ghost, r_ghost, v_end, r_end, x_end, v_in, r_in, x_in, own,
           p_out, p_got, q_out, q_got, ll_out, ll_got,
           load_sem, gap_sem, ll_sem, p_send, p_recv, q_send, q_recv):
    s = lax.axis_index("sub")
    has_left = s > 0
    has_right = s < lax.axis_size("sub") - 1
    c = cnt_ref[0, 0]
    final_slot = jnp.clip(c - 1, 0, SLOTS - 1)

    barrier = pltpu.get_barrier_semaphore()

    @pl.when(has_left)
    def _():
        pl.semaphore_signal(barrier, inc=1, device_id={"sub": s - 1}, device_id_type=pl.DeviceIdType.MESH)

    @pl.when(has_right)
    def _():
        pl.semaphore_signal(barrier, inc=1, device_id={"sub": s + 1}, device_id_type=pl.DeviceIdType.MESH)

    pairs_load = pltpu.make_async_copy(pairs_hbm.at[0, 0], pairs_ref, gap_sem.at[1])
    pairs_load.start()
    gap_load = pltpu.make_async_copy(gap_hbm.at[0, 0], gap, gap_sem.at[0])
    gap_load.start()
    loads = [pltpu.make_async_copy(ops_hbm.at[0, 0, j], ops.at[j], load_sem.at[j]) for j in range(SLOTS)]
    for load in loads:
        load.start()

    @pl.when(jnp.logical_not(has_left))
    def _():
        p_got[...] = jnp.zeros_like(p_got)

    @pl.when(jnp.logical_not(has_right))
    def _():
        q_got[...] = jnp.zeros_like(q_got)

    for ref in (v_ghost, r_ghost, v_end, r_end, x_end, own, far_out, w_far):
        ref[...] = jnp.zeros_like(ref)
    q_out[0] = jnp.zeros(q_out.shape[1:], F32)
    q_got[0] = jnp.zeros(q_got.shape[1:], F32)

    def p_copy(t, h):
        return pltpu.make_async_remote_copy(
            src_ref=p_out.at[t, h], dst_ref=p_got.at[t, h], send_sem=p_send.at[h], recv_sem=p_recv.at[t, h],
            device_id={"sub": s + 1}, device_id_type=pl.DeviceIdType.MESH)

    def q_copy(t, h):
        return pltpu.make_async_remote_copy(
            src_ref=q_out.at[t, h], dst_ref=q_got.at[t, h], send_sem=q_send.at[h], recv_sem=q_recv.at[t, h],
            device_id={"sub": s - 1}, device_id_type=pl.DeviceIdType.MESH)

    ll_copy = pltpu.make_async_remote_copy(
        src_ref=ll_out, dst_ref=ll_got, send_sem=ll_sem.at[0], recv_sem=ll_sem.at[1],
        device_id={"sub": s - 1}, device_id_type=pl.DeviceIdType.MESH)

    gap_load.wait()
    top = jnp.where(has_right, jnp.transpose(gap[final_slot]), 0.0)
    for h in range(CHUNKS):
        p_out[0, h] = -top[h * W:(h + 1) * W]
    for j in range(SLOTS - 1):
        turned_gap = jnp.where(j < c - 1, jnp.transpose(gap[j]), 0.0)
        for h in range(CHUNKS):
            r = turned_gap[h * W:(h + 1) * W]
            r_in[h, j] = r
            v_in[h, j] = r * (1.0 / CENTRE)
            x_in[h, j] = r * (1.0 / CENTRE)

    rows = lax.broadcasted_iota(jnp.int32, (H, H), 0)

    def selection(pairs):
        sign = jnp.where(pairs > 0, -1.0, 1.0)
        return jnp.where(rows == jnp.abs(pairs) - 1, sign, 0.0).astype(BF16)

    def turned(picked, block):
        high, low = halves(block)
        return nt(picked, high).astype(BF16), nt(picked, low).astype(BF16)

    def left_left(picked, j):
        high, low = turned(picked, ops[j, :H, :H])
        return nt(high, picked), nt(low, picked)

    def left_right(picked, j):
        high, low = halves(jnp.transpose(ops[j, :H, H:]))
        return nt(high, picked).astype(BF16), nt(low, picked).astype(BF16)

    pairs_load.wait()
    pairs = [pairs_ref[j:j + 1, :] for j in range(SLOTS)]
    loads[0].wait()
    picked = selection(pairs[0])
    ll_high, ll_low = left_left(picked, 0)
    ll_out[...] = ll_high + ll_low
    w_ll[0] = ll_high.astype(BF16)
    w_ll[1] = ll_low.astype(BF16)
    w_lr[0], w_lr[1] = left_right(picked, 0)

    for load in loads[1:]:
        load.wait()
    last_pairs = jnp.where(c == 1, pairs[0], jnp.where(c == 2, pairs[1], jnp.where(c == 3, pairs[2], pairs[3])))
    w_p[0, :H], w_p[1, :H] = turned(selection(last_pairs), ops[final_slot, H:, :H])
    w_p[0, H:], w_p[1, H:] = halves(jnp.transpose(ops[final_slot, H:, H:]))

    pl.semaphore_wait(barrier, has_left.astype(jnp.int32) + has_right.astype(jnp.int32))

    @pl.when(has_right)
    def _():
        for h in range(CHUNKS):
            p_copy(0, h).start()

    goes_first = lax.axis_index("grp") % 2 == 0

    @pl.when(jnp.logical_and(has_left, goes_first))
    def _():
        ll_copy.start()

    def product(x, w):
        high, low = x
        both = nn(jnp.concatenate([high, low], axis=0), w[0])
        return (both[:W] + both[W:]) + nn(high, w[1])

    def end_step(t, h, last):
        keep, add = chosen(KEEP, t), chosen(ADD, t)
        partial = p_out[t - 1, h] + far_out[h]

        @pl.when(jnp.logical_and(has_right, t > 1))
        def _():
            q_copy(t - 1, h).wait_recv()

        r = r_end[h] - jnp.where(has_right, partial + q_got[t - 1, h], 0.0)
        r_end[h] = r

        def rest():
            end = keep * v_end[h] + add * r
            q_out[t, h] = product(halves(jnp.where(c == 1, end, v_in[h, 0])), w_lr)

            @pl.when(has_left)
            def _():
                @pl.when(t > 1)
                def _():
                    q_copy(t - 1, h).wait_send()

                q_copy(t, h).start()

            v_end[h] = end
            x_end[h] = x_end[h] + end
            far_out[h] = product(halves(end), w_far)

        if last:
            pl.when(t <= ITERS)(rest)
        else:
            rest()

    def late_far():
        @pl.when(has_right)
        def _():
            ll_copy.wait_recv()
            w_far[0], w_far[1] = halves(ll_got[...])
            for h in range(CHUNKS):
                far_out[h] = product(halves(v_end[h]), w_far)

    def row(t, h, j):
        y = product((vb[h, :W, j * H:(j + 3) * H], vb[h, W:, j * H:(j + 3) * H]), w_in.at[j])
        r = r_in[h, j] - jnp.where(j < c - 1, y, 0.0)
        v = v_in[h, j]
        v = chosen(KEEP, t + 1) * v + chosen(ADD, t + 1) * r
        r_in[h, j] = r
        v_in[h, j] = v
        x_in[h, j] = x_in[h, j] + v

    def ghost_step(t, h):
        keep, add = chosen(KEEP, t), chosen(ADD, t)
        partial = q_out[t - 1, h] + own[h]
        inner = [v_in[h, j] for j in range(3)]
        end = v_end[h]

        @pl.when(has_left)
        def _():
            p_copy(t - 1, h).wait_recv()

        r = r_ghost[h] - jnp.where(has_left, partial + p_got[t - 1, h], 0.0)
        ghost = keep * v_ghost[h] + add * r
        before = jnp.where(c == 1, ghost, jnp.where(c == 2, inner[0], jnp.where(c == 3, inner[1], inner[2])))
        end_high, end_low = halves(end)
        high, low = halves(before)
        p_out[t, h] = product((jnp.concatenate([high, end_high], axis=1), jnp.concatenate([low, end_low], axis=1)), w_p)

        @pl.when(has_right)
        def _():
            p_copy(t - 1, h).wait_send()

            @pl.when(t < ITERS)
            def _():
                p_copy(t, h).start()

        r_ghost[h] = r
        v_ghost[h] = ghost
        for i, block in enumerate([ghost] + [jnp.where(c == j + 1, end, inner[j]) for j in range(3)] + [end]):
            high, low = halves(block)
            vb[h, :W, i * H:(i + 1) * H] = high
            vb[h, W:, i * H:(i + 1) * H] = low
        row(t, h, 0)

    def inner_step(t, h):
        row(t, h, 1)
        row(t, h, 2)
        own[h] = product((vb[h, :W, :H], vb[h, W:, :H]), w_ll)

    left_is_far = s % far == 0

    @pl.when(left_is_far)
    def _():
        @pl.loop(0, CHUNKS)
        def _(h):
            end_step(1, h, False)

    for j in range(SLOTS):
        picked = selection(pairs[j])
        if j > 0:
            ll_high, ll_low = left_left(picked, j)
            mid_high, mid_low = halves(jnp.transpose(ops[j - 1, H:, H:]) + (ll_high + ll_low))
            w_in[j - 1, 0, H:2 * H] = mid_high
            w_in[j - 1, 1, H:2 * H] = mid_low
            w_in[j - 1, 0, 2 * H:], w_in[j - 1, 1, 2 * H:] = left_right(picked, j)
        if j < SLOTS - 1:
            w_in[j, 0, :H], w_in[j, 1, :H] = turned(picked, ops[j, H:, :H])

    @pl.when(jnp.logical_and(has_left, jnp.logical_not(goes_first)))
    def _():
        ll_copy.start()

    def placed(inner, end, j):
        kept = jnp.where(j < c - 1, inner, 0.0) if j < 3 else jnp.zeros_like(end)
        return jnp.transpose(jnp.where(c - 1 == j, end, kept))

    def finish_x():
        end = x_end[...].reshape(RHS, H)
        for j in range(SLOTS):
            out_x[0, 0, j] = placed(x_in[:, j % 3].reshape(RHS, H), end, j)

    @pl.when(left_is_far)
    def _():
        late_far()

        @pl.loop(0, ITERS * CHUNKS)
        def _(n):
            t, h = n // CHUNKS + 1, n % CHUNKS
            pl.when(n == ITERS * CHUNKS - 1)(finish_x)
            ghost_step(t, h)
            end_step(t + 1, h, True)
            inner_step(t, h)

    @pl.when(jnp.logical_not(left_is_far))
    def _():
        @pl.loop(0, ITERS * CHUNKS)
        def _(n):
            t, h = n // CHUNKS + 1, n % CHUNKS
            end_step(t, h, False)
            pl.when(n == ITERS * CHUNKS - 1)(finish_x)
            ghost_step(t, h)
            inner_step(t, h)
            pl.when(n == CHUNKS - 1)(late_far)

    end = jnp.zeros((RHS, H), F32)
    for j in range(SLOTS):
        out_r[0, 0, j] = placed(r_in[:, j % 3].reshape(RHS, H), end, j)

    @pl.when(jnp.logical_and(jnp.logical_not(left_is_far), has_right))
    def _():
        @pl.loop(0, CHUNKS)
        def _(h):
            q_copy(ITERS, h).wait_recv()
            r_end[h] = r_end[h] - (p_out[ITERS, h] + far_out[h] + q_got[ITERS, h])

    end = jnp.transpose(r_end[...].reshape(RHS, H))
    for j in range(SLOTS):
        out_r[0, 0, j] = jnp.where(c - 1 == j, end, out_r[0, 0, j])

    @pl.when(has_left)
    def _():
        ll_copy.wait_send()
        for h in range(CHUNKS):
            q_copy(ITERS, h).wait_send()


def put_out(x, r, out_x, out_r, sems):
    stores = [pltpu.make_async_copy(x, out_x, sems.at[0]), pltpu.make_async_copy(r, out_r, sems.at[1])]
    for store in stores:
        store.start()
    for store in stores:
        store.wait()


def shards(far, operators, counts, pair_rows, gap):
    hbm = pl.BlockSpec(memory_space=pltpu.HBM)
    vmem = pl.BlockSpec(memory_space=pltpu.VMEM)
    dma = pltpu.SemaphoreType.DMA
    message = pltpu.VMEM((ITERS + 1, CHUNKS, W, H), F32)
    chunk = pltpu.VMEM((CHUNKS, W, H), F32)
    inner = pltpu.VMEM((CHUNKS, 3, W, H), F32)
    operator = pltpu.VMEM((2, H, H), BF16)
    block = jax.ShapeDtypeStruct((1, 1, SLOTS, H, RHS), F32)
    results = pl.pallas_call(
        functools.partial(kernel, far),
        out_shape=(block, block),
        in_specs=[pl.BlockSpec(memory_space=pltpu.SMEM), hbm, hbm, hbm],
        out_specs=(vmem, vmem),
        scratch_shapes=[
            pltpu.VMEM((SLOTS, M, M), F32),
            pltpu.VMEM((SLOTS, H, RHS), F32),
            pltpu.VMEM((SLOTS, H), jnp.int32),
            pltpu.VMEM((3, 2, 3 * H, H), BF16),
            pltpu.VMEM((2, 2 * H, H), BF16),
            operator,
            operator,
            operator,
            pltpu.VMEM((CHUNKS, 2 * W, 5 * H), BF16),
            chunk, chunk, chunk, chunk, chunk, chunk,
            inner, inner, inner,
            chunk,
            message, message, message, message,
            pltpu.VMEM((H, H), F32),
            pltpu.VMEM((H, H), F32),
            dma((SLOTS,)),
            dma((2,)),
            dma((2,)),
            dma((CHUNKS,)),
            dma((ITERS + 1, CHUNKS)),
            dma((CHUNKS,)),
            dma((ITERS + 1, CHUNKS)),
        ],
        compiler_params=pltpu.CompilerParams(
            collective_id=0, has_side_effects=True, vmem_limit_bytes=55_200_000),
        name="feti_chebyshev",
    )(counts, pair_rows, operators, gap)
    return pl.pallas_call(
        put_out,
        out_shape=(block, block),
        in_specs=[vmem, vmem],
        out_specs=(hbm, hbm),
        scratch_shapes=[dma((2,))],
        compiler_params=pltpu.CompilerParams(vmem_limit_bytes=8 * 1024 * 1024),
        name="put_out",
    )(*results)


def solution(mesh):
    return jax.shard_map(
        functools.partial(shards, 16 if mesh.shape["sub"] % 16 == 0 else 2),
        mesh=mesh,
        in_specs=(
            P("grp", "sub", None, None, None),
            P("grp", "sub"),
            P("grp", "sub", None, None),
            P("grp", "sub", None, None, None),
        ),
        out_specs=(P("grp", "sub", None, None, None), P("grp", "sub", None, None, None)),
        check_vma=False,
    )
```

```python
import functools

import jax
import jax.numpy as jnp
from jax import lax
from jax.experimental import pallas as pl
from jax.experimental.pallas import tpu as pltpu
from jax.sharding import PartitionSpec as P

M = 512
H = 256
RHS = 128
SLOTS = 4
ITERS = 6
CHUNKS = 2
W = RHS // CHUNKS

LOWER = 1.0
UPPER = 14.0
CENTRE = (UPPER + LOWER) / 2.0
RADIUS = (UPPER - LOWER) / 2.0

F32 = jnp.float32
BF16 = jnp.bfloat16


def coefficients():
    spread = CENTRE / RADIUS
    rho = 1.0 / spread
    keep, add = {1: 0.0}, {1: 1.0 / CENTRE}
    for t in range(2, ITERS + 1):
        new = 1.0 / (2.0 * spread - rho)
        keep[t] = new * rho
        add[t] = 2.0 * new / RADIUS
        rho = new
    keep[ITERS + 1] = add[ITERS + 1] = 0.0
    return keep, add


KEEP, ADD = coefficients()


def chosen(table, t):
    value = jnp.float32(table[ITERS + 1])
    for k in range(1, ITERS + 1):
        value = jnp.where(t == k, jnp.float32(table[k]), value)
    return value


def halves(x):
    high = x.astype(BF16)
    low = (x - high.astype(F32)).astype(BF16)
    return high, low


def nn(a, b):
    return jnp.dot(a, b, preferred_element_type=F32)


def nt(a, b):
    return lax.dot_general(a, b, (((1,), (1,)), ((), ())), preferred_element_type=F32)


def kernel(far, cnt_ref, pairs_hbm, ops_hbm, gap_hbm, out_x, out_r,
           ops, gap, pairs_ref, w_in, w_p, w_ll, w_lr, w_far, vb, far_out, pg_out, pl_out, row_out, before_in, v_ghost, r_ghost, v_end, r_end, x_end, v_in, r_in, x_in, own,
           p_out, p_got, q_out, q_got, ll_out, ll_got,
           load_sem, gap_sem, ll_sem, p_send, p_recv, q_send, q_recv):
    s = lax.axis_index("sub")
    has_left = s > 0
    has_right = s < lax.axis_size("sub") - 1
    left_is_far = s % far == 0
    right_is_far = s % far == far - 1
    both_near = jnp.logical_not(jnp.logical_or(left_is_far, right_is_far))
    c = cnt_ref[0, 0]
    final_slot = jnp.clip(c - 1, 0, SLOTS - 1)

    barrier = pltpu.get_barrier_semaphore()

    @pl.when(has_left)
    def _():
        pl.semaphore_signal(barrier, inc=1, device_id={"sub": s - 1}, device_id_type=pl.DeviceIdType.MESH)

    @pl.when(has_right)
    def _():
        pl.semaphore_signal(barrier, inc=1, device_id={"sub": s + 1}, device_id_type=pl.DeviceIdType.MESH)

    pairs_load = pltpu.make_async_copy(pairs_hbm.at[0, 0], pairs_ref, gap_sem.at[1])
    pairs_load.start()
    gap_load = pltpu.make_async_copy(gap_hbm.at[0, 0], gap, gap_sem.at[0])
    gap_load.start()
    loads = [pltpu.make_async_copy(ops_hbm.at[0, 0, j], ops.at[j], load_sem.at[j]) for j in range(SLOTS)]
    for load in loads:
        load.start()

    @pl.when(jnp.logical_not(has_left))
    def _():
        p_got[...] = jnp.zeros_like(p_got)

    @pl.when(jnp.logical_not(has_right))
    def _():
        q_got[...] = jnp.zeros_like(q_got)

    for ref in (v_ghost, r_ghost, v_end, r_end, x_end, own, far_out, w_far):
        ref[...] = jnp.zeros_like(ref)
    q_out[0] = jnp.zeros(q_out.shape[1:], F32)
    q_got[0] = jnp.zeros(q_got.shape[1:], F32)

    def p_copy(t, h):
        return pltpu.make_async_remote_copy(
            src_ref=p_out.at[t, h], dst_ref=p_got.at[t, h], send_sem=p_send.at[h], recv_sem=p_recv.at[t, h],
            device_id={"sub": s + 1}, device_id_type=pl.DeviceIdType.MESH)

    def q_copy(t, h):
        return pltpu.make_async_remote_copy(
            src_ref=q_out.at[t, h], dst_ref=q_got.at[t, h], send_sem=q_send.at[h], recv_sem=q_recv.at[t, h],
            device_id={"sub": s - 1}, device_id_type=pl.DeviceIdType.MESH)

    ll_copy = pltpu.make_async_remote_copy(
        src_ref=ll_out, dst_ref=ll_got, send_sem=ll_sem.at[0], recv_sem=ll_sem.at[1],
        device_id={"sub": s - 1}, device_id_type=pl.DeviceIdType.MESH)

    gap_load.wait()
    top = jnp.where(has_right, jnp.transpose(gap[final_slot]), 0.0)
    for h in range(CHUNKS):
        p_out[0, h] = -top[h * W:(h + 1) * W]

    def open_gate():
        pl.semaphore_wait(barrier, has_left.astype(jnp.int32) + has_right.astype(jnp.int32))

        @pl.when(has_right)
        def _():
            for h in range(CHUNKS):
                p_copy(0, h).start()

    pl.when(both_near)(open_gate)

    for j in range(SLOTS - 1):
        turned_gap = jnp.where(j < c - 1, jnp.transpose(gap[j]), 0.0)
        for h in range(CHUNKS):
            r = turned_gap[h * W:(h + 1) * W]
            r_in[h, j] = r
            v_in[h, j] = r * (1.0 / CENTRE)
            x_in[h, j] = r * (1.0 / CENTRE)

    rows = lax.broadcasted_iota(jnp.int32, (H, H), 0)

    def selection(pairs):
        sign = jnp.where(pairs > 0, -1.0, 1.0)
        return jnp.where(rows == jnp.abs(pairs) - 1, sign, 0.0).astype(BF16)

    def turned(picked, block):
        high, low = halves(block)
        return nt(picked, high).astype(BF16), nt(picked, low).astype(BF16)

    def left_left(picked, j):
        high, low = turned(picked, ops[j, :H, :H])
        return nt(high, picked), nt(low, picked)

    def left_right(picked, j):
        high, low = halves(jnp.transpose(ops[j, :H, H:]))
        return nt(high, picked).astype(BF16), nt(low, picked).astype(BF16)

    pairs_load.wait()
    pairs = [pairs_ref[j:j + 1, :] for j in range(SLOTS)]
    loads[0].wait()
    picked = selection(pairs[0])
    ll_high, ll_low = left_left(picked, 0)
    ll_out[...] = ll_high + ll_low
    w_ll[0] = ll_high.astype(BF16)
    w_ll[1] = ll_low.astype(BF16)
    w_lr[0], w_lr[1] = left_right(picked, 0)

    for load in loads[1:]:
        load.wait()
    last_pairs = jnp.where(c == 1, pairs[0], jnp.where(c == 2, pairs[1], jnp.where(c == 3, pairs[2], pairs[3])))
    w_p[0, :H], w_p[1, :H] = turned(selection(last_pairs), ops[final_slot, H:, :H])
    w_p[0, H:], w_p[1, H:] = halves(jnp.transpose(ops[final_slot, H:, H:]))

    pl.when(jnp.logical_not(both_near))(open_gate)

    goes_first = lax.axis_index("grp") % 2 == 0

    @pl.when(jnp.logical_and(has_left, goes_first))
    def _():
        ll_copy.start()

    def product(x, w):
        both = nn(jnp.concatenate(x, axis=0), w[0])
        return (both[:W] + both[W:]) + nn(x[0], w[1])

    def send_p(t, h):
        @pl.when(has_right)
        def _():
            p_copy(t - 1, h).wait_send()

            @pl.when(t < ITERS)
            def _():
                p_copy(t, h).start()

    def end_part(t, h, sends_p=False, guarded=False):
        keep, add = chosen(KEEP, t), chosen(ADD, t)
        partial = p_out[t - 1, h] + far_out[h]
        first = v_in[h, 0]

        @pl.when(jnp.logical_and(has_right, t > 1))
        def _():
            q_copy(t - 1, h).wait_recv()

        r = r_end[h] - jnp.where(has_right, partial + q_got[t - 1, h], 0.0)
        r_end[h] = r

        def rest():
            end = keep * v_end[h] + add * r
            split = halves(end)
            if sends_p:
                p_out[t, h] = pg_out[h] + product(split, (w_p[0, H:], w_p[1, H:]))
                send_p(t, h)
            q_out[t, h] = product(halves(jnp.where(c == 1, end, first)), w_lr)

            @pl.when(has_left)
            def _():
                @pl.when(t > 1)
                def _():
                    q_copy(t - 1, h).wait_send()

                q_copy(t, h).start()

            if not sends_p:
                pl_out[h] = product(split, (w_p[0, H:], w_p[1, H:]))
            v_end[h] = end
            x_end[h] = x_end[h] + end
            far_out[h] = product(split, w_far)
            if guarded:
                heavy_part(t, h, False)

        if guarded:
            pl.when(t <= ITERS)(rest)
        else:
            rest()

    def late_far():
        @pl.when(has_right)
        def _():
            ll_copy.wait_recv()
            w_far[0], w_far[1] = halves(ll_got[...])
            for h in range(CHUNKS):
                far_out[h] = product(halves(v_end[h]), w_far)

    def advance(t, h, j, y):
        r = r_in[h, j] - jnp.where(j < c - 1, y, 0.0)
        v = chosen(KEEP, t + 1) * v_in[h, j] + chosen(ADD, t + 1) * r
        r_in[h, j] = r
        v_in[h, j] = v
        x_in[h, j] = x_in[h, j] + v

    def ghost_part(t, h, sends_p=True, held=False):
        keep, add = chosen(KEEP, t), chosen(ADD, t)
        partial = q_out[t - 1, h] + own[h]
        if held:
            before = before_in[h]
        else:
            before = jnp.where(c == 2, v_in[h, 0], jnp.where(c == 3, v_in[h, 1], v_in[h, 2]))

        @pl.when(has_left)
        def _():
            p_copy(t - 1, h).wait_recv()

        r = r_ghost[h] - jnp.where(has_left, partial + p_got[t - 1, h], 0.0)
        ghost = keep * v_ghost[h] + add * r
        split = halves(ghost)
        from_left = product(halves(jnp.where(c == 1, ghost, before)), (w_p[0, :H], w_p[1, :H]))
        if sends_p:
            p_out[t, h] = from_left + pl_out[h]
        else:
            pg_out[h] = from_left
        y = product(split, (w_in[0, 0, :H], w_in[0, 1, :H]))
        if held:
            advance(t, h, 0, y + row_out[h])
        else:
            row_out[h] = y
        r_ghost[h] = r
        v_ghost[h] = ghost
        if sends_p:
            send_p(t, h)
        own[h] = product(split, w_ll)

    def heavy_part(t, h, finishes):
        inner = [v_in[h, j] for j in range(3)]
        end = v_end[h]
        if not finishes:
            before_in[h] = jnp.where(c == 2, inner[0], jnp.where(c == 3, inner[1], inner[2]))
        blocks = [inner[0]] + [jnp.where(c == j + 1, end, inner[j]) for j in (1, 2)] + [end]
        for i, block in enumerate(blocks):
            high, low = halves(jnp.where(c == 1, end, block) if i == 0 else block)
            vb[h, 0, :, i * H:(i + 1) * H] = high
            vb[h, 1, :, i * H:(i + 1) * H] = low

        def columns(k, width):
            return vb[h, 0, :, k * H:(k + width) * H], vb[h, 1, :, k * H:(k + width) * H]

        y = product(columns(0, 2), (w_in[0, 0, H:], w_in[0, 1, H:]))
        if finishes:
            advance(t, h, 0, y + row_out[h])
        else:
            row_out[h] = y
        for j in (1, 2):
            advance(t, h, j, product(columns(j - 1, 3), w_in.at[j]))


    @pl.when(left_is_far)
    def _():
        @pl.loop(0, CHUNKS)
        def _(h):
            end_part(1, h)

    for j in range(SLOTS):
        picked = selection(pairs[j])
        if j > 0:
            ll_high, ll_low = left_left(picked, j)
            mid_high, mid_low = halves(jnp.transpose(ops[j - 1, H:, H:]) + (ll_high + ll_low))
            w_in[j - 1, 0, H:2 * H] = mid_high
            w_in[j - 1, 1, H:2 * H] = mid_low
            w_in[j - 1, 0, 2 * H:], w_in[j - 1, 1, 2 * H:] = left_right(picked, j)
        if j < SLOTS - 1:
            w_in[j, 0, :H], w_in[j, 1, :H] = turned(picked, ops[j, H:, :H])

    @pl.when(jnp.logical_and(has_left, jnp.logical_not(goes_first)))
    def _():
        ll_copy.start()

    def placed(inner, end, j):
        kept = jnp.where(j < c - 1, inner, 0.0) if j < 3 else jnp.zeros_like(end)
        return jnp.transpose(jnp.where(c - 1 == j, end, kept))

    def finish_x():
        end = x_end[...].reshape(RHS, H)
        for j in range(SLOTS):
            out_x[0, 0, j] = placed(x_in[:, j % 3].reshape(RHS, H), end, j)

    def all_steps(body):
        @pl.loop(0, ITERS * CHUNKS)
        def _(n):
            body(n // CHUNKS + 1, n % CHUNKS, n)

    last = ITERS * CHUNKS - 1

    @pl.when(left_is_far)
    def _():
        @pl.loop(0, CHUNKS)
        def _(h):
            heavy_part(1, h, False)

        late_far()

        @all_steps
        def _(t, h, n):
            pl.when(n == last)(finish_x)
            ghost_part(t, h, held=True)
            end_part(t + 1, h, guarded=True)

    @pl.when(right_is_far)
    def _():
        @all_steps
        def _(t, h, n):
            ghost_part(t, h, sends_p=False)
            end_part(t, h, sends_p=True)
            heavy_part(t, h, True)
            pl.when(n == CHUNKS - 1)(late_far)
            pl.when(n == last)(finish_x)

    @pl.when(both_near)
    def _():
        @all_steps
        def _(t, h, n):
            end_part(t, h)
            pl.when(n == last)(finish_x)
            ghost_part(t, h)
            heavy_part(t, h, True)
            pl.when(n == CHUNKS - 1)(late_far)

    end = jnp.zeros((RHS, H), F32)
    for j in range(SLOTS):
        out_r[0, 0, j] = placed(r_in[:, j % 3].reshape(RHS, H), end, j)

    @pl.when(jnp.logical_and(jnp.logical_not(left_is_far), has_right))
    def _():
        @pl.loop(0, CHUNKS)
        def _(h):
            q_copy(ITERS, h).wait_recv()
            r_end[h] = r_end[h] - (p_out[ITERS, h] + far_out[h] + q_got[ITERS, h])

    end = jnp.transpose(r_end[...].reshape(RHS, H))
    for j in range(SLOTS):
        out_r[0, 0, j] = jnp.where(c - 1 == j, end, out_r[0, 0, j])

    @pl.when(has_left)
    def _():
        ll_copy.wait_send()
        for h in range(CHUNKS):
            q_copy(ITERS, h).wait_send()


def put_out(x, r, out_x, out_r, sems):
    stores = [pltpu.make_async_copy(x, out_x, sems.at[0]), pltpu.make_async_copy(r, out_r, sems.at[1])]
    for store in stores:
        store.start()
    for store in stores:
        store.wait()


def shards(far, operators, counts, pair_rows, gap):
    hbm = pl.BlockSpec(memory_space=pltpu.HBM)
    vmem = pl.BlockSpec(memory_space=pltpu.VMEM)
    dma = pltpu.SemaphoreType.DMA
    message = pltpu.VMEM((ITERS + 1, CHUNKS, W, H), F32)
    chunk = pltpu.VMEM((CHUNKS, W, H), F32)
    inner = pltpu.VMEM((CHUNKS, 3, W, H), F32)
    operator = pltpu.VMEM((2, H, H), BF16)
    block = jax.ShapeDtypeStruct((1, 1, SLOTS, H, RHS), F32)
    results = pl.pallas_call(
        functools.partial(kernel, far),
        out_shape=(block, block),
        in_specs=[pl.BlockSpec(memory_space=pltpu.SMEM), hbm, hbm, hbm],
        out_specs=(vmem, vmem),
        scratch_shapes=[
            pltpu.VMEM((SLOTS, M, M), F32),
            pltpu.VMEM((SLOTS, H, RHS), F32),
            pltpu.VMEM((SLOTS, H), jnp.int32),
            pltpu.VMEM((3, 2, 3 * H, H), BF16),
            pltpu.VMEM((2, 2 * H, H), BF16),
            operator,
            operator,
            operator,
            pltpu.VMEM((CHUNKS, 2, W, 4 * H), BF16),
            chunk, chunk, chunk, chunk, chunk, chunk, chunk, chunk, chunk, chunk,
            inner, inner, inner,
            chunk,
            message, message, message, message,
            pltpu.VMEM((H, H), F32),
            pltpu.VMEM((H, H), F32),
            dma((SLOTS,)),
            dma((2,)),
            dma((2,)),
            dma((CHUNKS,)),
            dma((ITERS + 1, CHUNKS)),
            dma((CHUNKS,)),
            dma((ITERS + 1, CHUNKS)),
        ],
        compiler_params=pltpu.CompilerParams(
            collective_id=0, has_side_effects=True, vmem_limit_bytes=55_200_000),
        name="feti_chebyshev",
    )(counts, pair_rows, operators, gap)
    return pl.pallas_call(
        put_out,
        out_shape=(block, block),
        in_specs=[vmem, vmem],
        out_specs=(hbm, hbm),
        scratch_shapes=[dma((2,))],
        compiler_params=pltpu.CompilerParams(vmem_limit_bytes=8 * 1024 * 1024),
        name="put_out",
    )(*results)


def solution(mesh):
    return jax.shard_map(
        functools.partial(shards, 16 if mesh.shape["sub"] % 16 == 0 else 2),
        mesh=mesh,
        in_specs=(
            P("grp", "sub", None, None, None),
            P("grp", "sub"),
            P("grp", "sub", None, None),
            P("grp", "sub", None, None, None),
        ),
        out_specs=(P("grp", "sub", None, None, None), P("grp", "sub", None, None, None)),
        check_vma=False,
    )
```

```python
import functools

import jax
import jax.numpy as jnp
from jax import lax
from jax.experimental import pallas as pl
from jax.experimental.pallas import tpu as pltpu
from jax.sharding import PartitionSpec as P

M = 512
H = 256
RHS = 128
SLOTS = 4
ITERS = 6
CHUNKS = 2
W = RHS // CHUNKS

LOWER = 1.0
UPPER = 14.0
CENTRE = (UPPER + LOWER) / 2.0
RADIUS = (UPPER - LOWER) / 2.0

F32 = jnp.float32
BF16 = jnp.bfloat16


def coefficients():
    spread = CENTRE / RADIUS
    rho = 1.0 / spread
    keep, add = {1: 0.0}, {1: 1.0 / CENTRE}
    for t in range(2, ITERS + 1):
        new = 1.0 / (2.0 * spread - rho)
        keep[t] = new * rho
        add[t] = 2.0 * new / RADIUS
        rho = new
    keep[ITERS + 1] = add[ITERS + 1] = 0.0
    return keep, add


KEEP, ADD = coefficients()


def chosen(table, t):
    value = jnp.float32(table[ITERS + 1])
    for k in range(1, ITERS + 1):
        value = jnp.where(t == k, jnp.float32(table[k]), value)
    return value


def halves(x):
    high = x.astype(BF16)
    low = (x - high.astype(F32)).astype(BF16)
    return high, low


def nn(a, b):
    return jnp.dot(a, b, preferred_element_type=F32)


def nt(a, b):
    return lax.dot_general(a, b, (((1,), (1,)), ((), ())), preferred_element_type=F32)


def kernel(far, cnt_ref, pairs_hbm, ops_hbm, gap_hbm, out_x, out_r,
           ops, gap, pairs_ref, w_in, w_p, w_ll, w_lr, w_far, vb, far_out, pg_out, pl_out, row_out, before_in, v_ghost, r_ghost, v_end, r_end, x_end, v_in, r_in, x_in, own,
           p_out, p_got, q_out, q_got, ll_out, ll_got,
           load_sem, gap_sem, ll_sem, p_send, p_recv, q_send, q_recv):
    s = lax.axis_index("sub")
    has_left = s > 0
    has_right = s < lax.axis_size("sub") - 1
    left_is_far = s % far == 0
    right_is_far = s % far == far - 1
    both_near = jnp.logical_not(jnp.logical_or(left_is_far, right_is_far))
    c = cnt_ref[0, 0]
    final_slot = jnp.clip(c - 1, 0, SLOTS - 1)

    barrier = pltpu.get_barrier_semaphore()

    @pl.when(has_left)
    def _():
        pl.semaphore_signal(barrier, inc=1, device_id={"sub": s - 1}, device_id_type=pl.DeviceIdType.MESH)

    @pl.when(has_right)
    def _():
        pl.semaphore_signal(barrier, inc=1, device_id={"sub": s + 1}, device_id_type=pl.DeviceIdType.MESH)

    pairs_load = pltpu.make_async_copy(pairs_hbm.at[0, 0], pairs_ref, gap_sem.at[1])
    pairs_load.start()
    gap_load = pltpu.make_async_copy(gap_hbm.at[0, 0], gap, gap_sem.at[0])
    gap_load.start()
    loads = [pltpu.make_async_copy(ops_hbm.at[0, 0, j], ops.at[j], load_sem.at[j]) for j in range(SLOTS)]
    for load in loads:
        load.start()

    @pl.when(jnp.logical_not(has_left))
    def _():
        p_got[...] = jnp.zeros_like(p_got)

    @pl.when(jnp.logical_not(has_right))
    def _():
        q_got[...] = jnp.zeros_like(q_got)

    for ref in (v_ghost, r_ghost, v_end, r_end, x_end, own, far_out, w_far):
        ref[...] = jnp.zeros_like(ref)
    q_out[0] = jnp.zeros(q_out.shape[1:], F32)
    q_got[0] = jnp.zeros(q_got.shape[1:], F32)

    def p_copy(t, h):
        return pltpu.make_async_remote_copy(
            src_ref=p_out.at[t, h], dst_ref=p_got.at[t, h], send_sem=p_send.at[h], recv_sem=p_recv.at[t, h],
            device_id={"sub": s + 1}, device_id_type=pl.DeviceIdType.MESH)

    def q_copy(t, h):
        return pltpu.make_async_remote_copy(
            src_ref=q_out.at[t, h], dst_ref=q_got.at[t, h], send_sem=q_send.at[h], recv_sem=q_recv.at[t, h],
            device_id={"sub": s - 1}, device_id_type=pl.DeviceIdType.MESH)

    ll_copy = pltpu.make_async_remote_copy(
        src_ref=ll_out, dst_ref=ll_got, send_sem=ll_sem.at[0], recv_sem=ll_sem.at[1],
        device_id={"sub": s - 1}, device_id_type=pl.DeviceIdType.MESH)

    gap_load.wait()
    top = jnp.where(has_right, jnp.transpose(gap[final_slot]), 0.0)
    for h in range(CHUNKS):
        p_out[0, h] = -top[h * W:(h + 1) * W]

    def open_gate():
        pl.semaphore_wait(barrier, has_left.astype(jnp.int32) + has_right.astype(jnp.int32))

        @pl.when(has_right)
        def _():
            for h in range(CHUNKS):
                p_copy(0, h).start()

    pl.when(both_near)(open_gate)

    for j in range(SLOTS - 1):
        turned_gap = jnp.where(j < c - 1, jnp.transpose(gap[j]), 0.0)
        for h in range(CHUNKS):
            r = turned_gap[h * W:(h + 1) * W]
            r_in[h, j] = r
            v_in[h, j] = r * (1.0 / CENTRE)
            x_in[h, j] = r * (1.0 / CENTRE)

    rows = lax.broadcasted_iota(jnp.int32, (H, H), 0)

    def selection(pairs):
        sign = jnp.where(pairs > 0, -1.0, 1.0)
        return jnp.where(rows == jnp.abs(pairs) - 1, sign, 0.0).astype(BF16)

    def turned(picked, block):
        high, low = halves(block)
        return nt(picked, high).astype(BF16), nt(picked, low).astype(BF16)

    def left_left(picked, j):
        high, low = turned(picked, ops[j, :H, :H])
        return nt(high, picked), nt(low, picked)

    def left_right(picked, j):
        high, low = halves(jnp.transpose(ops[j, :H, H:]))
        return nt(high, picked).astype(BF16), nt(low, picked).astype(BF16)

    pairs_load.wait()
    pairs = [pairs_ref[j:j + 1, :] for j in range(SLOTS)]
    loads[0].wait()
    picked = selection(pairs[0])
    ll_high, ll_low = left_left(picked, 0)
    ll_out[...] = ll_high + ll_low
    w_ll[0] = ll_high.astype(BF16)
    w_ll[1] = ll_low.astype(BF16)
    w_lr[0], w_lr[1] = left_right(picked, 0)

    for load in loads[1:]:
        load.wait()
    last_pairs = jnp.where(c == 1, pairs[0], jnp.where(c == 2, pairs[1], jnp.where(c == 3, pairs[2], pairs[3])))
    w_p[0, :H], w_p[1, :H] = turned(selection(last_pairs), ops[final_slot, H:, :H])
    w_p[0, H:], w_p[1, H:] = halves(jnp.transpose(ops[final_slot, H:, H:]))

    pl.when(jnp.logical_not(both_near))(open_gate)

    sends_block = jnp.logical_and(has_left, left_is_far)
    goes_first = lax.axis_index("grp") % 2 == 0

    @pl.when(jnp.logical_and(sends_block, goes_first))
    def _():
        ll_copy.start()

    def product(x, w):
        both = nn(jnp.concatenate(x, axis=0), w[0])
        return (both[:W] + both[W:]) + nn(x[0], w[1])

    def send_p(t, h):
        @pl.when(has_right)
        def _():
            p_copy(t - 1, h).wait_send()

            @pl.when(t < ITERS)
            def _():
                p_copy(t, h).start()

    def send_q(t, h):
        @pl.when(has_left)
        def _():
            @pl.when(t > 1)
            def _():
                q_copy(t - 1, h).wait_send()

            q_copy(t, h).start()

    def end_part(t, h, left_far=False, right_far=False, guarded=False):
        keep, add = chosen(KEEP, t), chosen(ADD, t)
        partial = p_out[t - 1, h]
        if right_far:
            partial = partial + far_out[h]
        first = v_in[h, 0]

        @pl.when(jnp.logical_and(has_right, t > 1))
        def _():
            q_copy(t - 1, h).wait_recv()

        r = r_end[h] - jnp.where(has_right, partial + q_got[t - 1, h], 0.0)
        r_end[h] = r

        def rest():
            end = keep * v_end[h] + add * r
            split = halves(end)
            if right_far:
                p_out[t, h] = pg_out[h] + product(split, (w_p[0, H:], w_p[1, H:]))
                send_p(t, h)
            own_columns = product(halves(jnp.where(c == 1, end, first)), w_lr)
            if left_far:
                q_out[t, h] = own_columns
                send_q(t, h)
            elif right_far:
                q_out[t, h] = own_columns + own[h]
                send_q(t, h)
            else:
                own[h] = own_columns
            if right_far:
                far_out[h] = product(split, w_far)
            else:
                pl_out[h] = product(split, (w_p[0, H:], w_p[1, H:]))
            v_end[h] = end
            x_end[h] = x_end[h] + end
            if guarded:
                heavy_part(t, h, False)

        if guarded:
            pl.when(t <= ITERS)(rest)
        else:
            rest()

    def late_far():
        @pl.when(has_right)
        def _():
            ll_copy.wait_recv()
            w_far[0], w_far[1] = halves(ll_got[...])
            for h in range(CHUNKS):
                far_out[h] = product(halves(v_end[h]), w_far)

    def advance(t, h, j, y):
        r = r_in[h, j] - jnp.where(j < c - 1, y, 0.0)
        v = chosen(KEEP, t + 1) * v_in[h, j] + chosen(ADD, t + 1) * r
        r_in[h, j] = r
        v_in[h, j] = v
        x_in[h, j] = x_in[h, j] + v

    def ghost_part(t, h, left_far=False, right_far=False):
        keep, add = chosen(KEEP, t), chosen(ADD, t)
        partial = q_out[t - 1, h]
        if left_far:
            partial = partial + own[h]
            before = before_in[h]
        else:
            before = jnp.where(c == 2, v_in[h, 0], jnp.where(c == 3, v_in[h, 1], v_in[h, 2]))

        @pl.when(has_left)
        def _():
            p_copy(t - 1, h).wait_recv()

        r = r_ghost[h] - jnp.where(has_left, partial + p_got[t - 1, h], 0.0)
        ghost = keep * v_ghost[h] + add * r
        split = halves(ghost)
        from_left = product(halves(jnp.where(c == 1, ghost, before)), (w_p[0, :H], w_p[1, :H]))
        if right_far:
            pg_out[h] = from_left
        else:
            p_out[t, h] = from_left + pl_out[h]
        if left_far:
            advance(t, h, 0, product(split, (w_in[0, 0, :H], w_in[0, 1, :H])) + row_out[h])
            send_p(t, h)
            own[h] = product(split, w_ll)
        elif right_far:
            own[h] = product(split, w_ll)
            row_out[h] = product(split, (w_in[0, 0, :H], w_in[0, 1, :H]))
        else:
            q_out[t, h] = product(split, w_ll) + own[h]
            send_p(t, h)
            send_q(t, h)
            row_out[h] = product(split, (w_in[0, 0, :H], w_in[0, 1, :H]))
        r_ghost[h] = r
        v_ghost[h] = ghost

    def heavy_part(t, h, finishes):
        inner = [v_in[h, j] for j in range(3)]
        end = v_end[h]
        if not finishes:
            before_in[h] = jnp.where(c == 2, inner[0], jnp.where(c == 3, inner[1], inner[2]))
        blocks = [inner[0]] + [jnp.where(c == j + 1, end, inner[j]) for j in (1, 2)] + [end]
        for i, block in enumerate(blocks):
            high, low = halves(jnp.where(c == 1, end, block) if i == 0 else block)
            vb[h, 0, :, i * H:(i + 1) * H] = high
            vb[h, 1, :, i * H:(i + 1) * H] = low

        def columns(k, width):
            return vb[h, 0, :, k * H:(k + width) * H], vb[h, 1, :, k * H:(k + width) * H]

        y = product(columns(0, 2), (w_in[0, 0, H:], w_in[0, 1, H:]))
        if finishes:
            advance(t, h, 0, y + row_out[h])
        else:
            row_out[h] = y
        for j in (1, 2):
            advance(t, h, j, product(columns(j - 1, 3), w_in.at[j]))


    @pl.when(left_is_far)
    def _():
        @pl.loop(0, CHUNKS)
        def _(h):
            end_part(1, h, left_far=True)

    for j in range(SLOTS):
        picked = selection(pairs[j])
        if j > 0:
            ll_high, ll_low = left_left(picked, j)
            mid_high, mid_low = halves(jnp.transpose(ops[j - 1, H:, H:]) + (ll_high + ll_low))
            w_in[j - 1, 0, H:2 * H] = mid_high
            w_in[j - 1, 1, H:2 * H] = mid_low
            w_in[j - 1, 0, 2 * H:], w_in[j - 1, 1, 2 * H:] = left_right(picked, j)
        if j < SLOTS - 1:
            w_in[j, 0, :H], w_in[j, 1, :H] = turned(picked, ops[j, H:, :H])

    @pl.when(jnp.logical_and(sends_block, jnp.logical_not(goes_first)))
    def _():
        ll_copy.start()

    def placed(inner, end, j):
        kept = jnp.where(j < c - 1, inner, 0.0) if j < 3 else jnp.zeros_like(end)
        return jnp.transpose(jnp.where(c - 1 == j, end, kept))

    def finish_x():
        end = x_end[...].reshape(RHS, H)
        for j in range(SLOTS):
            out_x[0, 0, j] = placed(x_in[:, j % 3].reshape(RHS, H), end, j)

    def all_steps(body):
        @pl.loop(0, ITERS * CHUNKS)
        def _(n):
            body(n // CHUNKS + 1, n % CHUNKS, n)

    last = ITERS * CHUNKS - 1

    @pl.when(left_is_far)
    def _():
        @pl.loop(0, CHUNKS)
        def _(h):
            heavy_part(1, h, False)

        @all_steps
        def _(t, h, n):
            pl.when(n == last)(finish_x)
            ghost_part(t, h, left_far=True)
            end_part(t + 1, h, left_far=True, guarded=True)

    @pl.when(right_is_far)
    def _():
        @all_steps
        def _(t, h, n):
            ghost_part(t, h, right_far=True)
            end_part(t, h, right_far=True)
            heavy_part(t, h, True)
            pl.when(n == CHUNKS - 1)(late_far)
            pl.when(n == last)(finish_x)

    @pl.when(both_near)
    def _():
        @all_steps
        def _(t, h, n):
            end_part(t, h)
            pl.when(n == last)(finish_x)
            ghost_part(t, h)
            heavy_part(t, h, True)

    end = jnp.zeros((RHS, H), F32)
    for j in range(SLOTS):
        out_r[0, 0, j] = placed(r_in[:, j % 3].reshape(RHS, H), end, j)

    @pl.when(jnp.logical_and(jnp.logical_not(left_is_far), has_right))
    def _():
        @pl.loop(0, CHUNKS)
        def _(h):
            q_copy(ITERS, h).wait_recv()
            r_end[h] = r_end[h] - ((p_out[ITERS, h] + q_got[ITERS, h]) + jnp.where(right_is_far, far_out[h], 0.0))

    end = jnp.transpose(r_end[...].reshape(RHS, H))
    for j in range(SLOTS):
        out_r[0, 0, j] = jnp.where(c - 1 == j, end, out_r[0, 0, j])

    pl.when(sends_block)(ll_copy.wait_send)

    @pl.when(has_left)
    def _():
        for h in range(CHUNKS):
            q_copy(ITERS, h).wait_send()


def put_out(x, r, out_x, out_r, sems):
    stores = [pltpu.make_async_copy(x, out_x, sems.at[0]), pltpu.make_async_copy(r, out_r, sems.at[1])]
    for store in stores:
        store.start()
    for store in stores:
        store.wait()


def shards(far, operators, counts, pair_rows, gap):
    hbm = pl.BlockSpec(memory_space=pltpu.HBM)
    vmem = pl.BlockSpec(memory_space=pltpu.VMEM)
    dma = pltpu.SemaphoreType.DMA
    message = pltpu.VMEM((ITERS + 1, CHUNKS, W, H), F32)
    chunk = pltpu.VMEM((CHUNKS, W, H), F32)
    inner = pltpu.VMEM((CHUNKS, 3, W, H), F32)
    operator = pltpu.VMEM((2, H, H), BF16)
    block = jax.ShapeDtypeStruct((1, 1, SLOTS, H, RHS), F32)
    results = pl.pallas_call(
        functools.partial(kernel, far),
        out_shape=(block, block),
        in_specs=[pl.BlockSpec(memory_space=pltpu.SMEM), hbm, hbm, hbm],
        out_specs=(vmem, vmem),
        scratch_shapes=[
            pltpu.VMEM((SLOTS, M, M), F32),
            pltpu.VMEM((SLOTS, H, RHS), F32),
            pltpu.VMEM((SLOTS, H), jnp.int32),
            pltpu.VMEM((3, 2, 3 * H, H), BF16),
            pltpu.VMEM((2, 2 * H, H), BF16),
            operator,
            operator,
            operator,
            pltpu.VMEM((CHUNKS, 2, W, 4 * H), BF16),
            chunk, chunk, chunk, chunk, chunk, chunk, chunk, chunk, chunk, chunk,
            inner, inner, inner,
            chunk,
            message, message, message, message,
            pltpu.VMEM((H, H), F32),
            pltpu.VMEM((H, H), F32),
            dma((SLOTS,)),
            dma((2,)),
            dma((2,)),
            dma((CHUNKS,)),
            dma((ITERS + 1, CHUNKS)),
            dma((CHUNKS,)),
            dma((ITERS + 1, CHUNKS)),
        ],
        compiler_params=pltpu.CompilerParams(
            collective_id=0, has_side_effects=True, vmem_limit_bytes=55_200_000),
        name="feti_chebyshev",
    )(counts, pair_rows, operators, gap)
    return pl.pallas_call(
        put_out,
        out_shape=(block, block),
        in_specs=[vmem, vmem],
        out_specs=(hbm, hbm),
        scratch_shapes=[dma((2,))],
        compiler_params=pltpu.CompilerParams(vmem_limit_bytes=8 * 1024 * 1024),
        name="put_out",
    )(*results)


def solution(mesh):
    return jax.shard_map(
        functools.partial(shards, 16 if mesh.shape["sub"] % 16 == 0 else 2),
        mesh=mesh,
        in_specs=(
            P("grp", "sub", None, None, None),
            P("grp", "sub"),
            P("grp", "sub", None, None),
            P("grp", "sub", None, None, None),
        ),
        out_specs=(P("grp", "sub", None, None, None), P("grp", "sub", None, None, None)),
        check_vma=False,
    )
```

```python
import functools

import jax
import jax.numpy as jnp
from jax import lax
from jax.experimental import pallas as pl
from jax.experimental.pallas import tpu as pltpu
from jax.sharding import PartitionSpec as P

M = 512
H = 256
RHS = 128
SLOTS = 4
ITERS = 6
CHUNKS = 2
W = RHS // CHUNKS

LOWER = 1.0
UPPER = 14.0
CENTRE = (UPPER + LOWER) / 2.0
RADIUS = (UPPER - LOWER) / 2.0

F32 = jnp.float32
BF16 = jnp.bfloat16


def coefficients():
    spread = CENTRE / RADIUS
    rho = 1.0 / spread
    keep, add = {1: 0.0}, {1: 1.0 / CENTRE}
    for t in range(2, ITERS + 1):
        new = 1.0 / (2.0 * spread - rho)
        keep[t] = new * rho
        add[t] = 2.0 * new / RADIUS
        rho = new
    keep[ITERS + 1] = add[ITERS + 1] = 0.0
    return keep, add


KEEP, ADD = coefficients()


def chosen(table, t):
    value = jnp.float32(table[ITERS + 1])
    for k in range(1, ITERS + 1):
        value = jnp.where(t == k, jnp.float32(table[k]), value)
    return value


def halves(x):
    high = x.astype(BF16)
    low = (x - high.astype(F32)).astype(BF16)
    return high, low


def nn(a, b):
    return jnp.dot(a, b, preferred_element_type=F32)


def nt(a, b):
    return lax.dot_general(a, b, (((1,), (1,)), ((), ())), preferred_element_type=F32)


def kernel(far, cnt_ref, pairs_hbm, ops_hbm, gap_hbm, out_x, out_r,
           ops, gap, pairs_ref, w_in, w_p, w_ll, w_lr, w_far, vb, far_out, pg_out, pl_out, row_out, before_in, v_ghost, r_ghost, v_end, r_end, x_end, v_in, r_in, x_in, own,
           p_out, p_got, q_out, q_got, ll_out, ll_got,
           load_sem, gap_sem, ll_sem, p_send, p_recv, q_send, q_recv):
    s = lax.axis_index("sub")
    has_left = s > 0
    has_right = s < lax.axis_size("sub") - 1
    left_is_far = s % far == 0
    right_is_far = s % far == far - 1
    both_near = jnp.logical_not(jnp.logical_or(left_is_far, right_is_far))
    c = cnt_ref[0, 0]
    final_slot = jnp.clip(c - 1, 0, SLOTS - 1)

    barrier = pltpu.get_barrier_semaphore()

    @pl.when(has_left)
    def _():
        pl.semaphore_signal(barrier, inc=1, device_id={"sub": s - 1}, device_id_type=pl.DeviceIdType.MESH)

    @pl.when(has_right)
    def _():
        pl.semaphore_signal(barrier, inc=1, device_id={"sub": s + 1}, device_id_type=pl.DeviceIdType.MESH)

    pairs_load = pltpu.make_async_copy(pairs_hbm.at[0, 0], pairs_ref, gap_sem.at[1])
    pairs_load.start()
    gap_load = pltpu.make_async_copy(gap_hbm.at[0, 0], gap, gap_sem.at[0])
    gap_load.start()
    loads = [pltpu.make_async_copy(ops_hbm.at[0, 0, j], ops.at[j], load_sem.at[j]) for j in range(SLOTS)]
    for load in loads:
        load.start()

    @pl.when(jnp.logical_not(has_left))
    def _():
        p_got[...] = jnp.zeros_like(p_got)

    @pl.when(jnp.logical_not(has_right))
    def _():
        q_got[...] = jnp.zeros_like(q_got)

    for ref in (v_ghost, r_ghost, v_end, r_end, x_end, own, far_out, w_far):
        ref[...] = jnp.zeros_like(ref)
    q_out[0] = jnp.zeros(q_out.shape[1:], F32)
    q_got[0] = jnp.zeros(q_got.shape[1:], F32)

    def p_copy(t, h):
        return pltpu.make_async_remote_copy(
            src_ref=p_out.at[t, h], dst_ref=p_got.at[t, h], send_sem=p_send.at[h], recv_sem=p_recv.at[t, h],
            device_id={"sub": s + 1}, device_id_type=pl.DeviceIdType.MESH)

    def q_copy(t, h):
        return pltpu.make_async_remote_copy(
            src_ref=q_out.at[t, h], dst_ref=q_got.at[t, h], send_sem=q_send.at[h], recv_sem=q_recv.at[t, h],
            device_id={"sub": s - 1}, device_id_type=pl.DeviceIdType.MESH)

    ll_copy = pltpu.make_async_remote_copy(
        src_ref=ll_out, dst_ref=ll_got, send_sem=ll_sem.at[0], recv_sem=ll_sem.at[1],
        device_id={"sub": s - 1}, device_id_type=pl.DeviceIdType.MESH)

    gap_load.wait()
    top = jnp.where(has_right, jnp.transpose(gap[final_slot]), 0.0)
    for h in range(CHUNKS):
        p_out[0, h] = -top[h * W:(h + 1) * W]

    def open_gate():
        pl.semaphore_wait(barrier, has_left.astype(jnp.int32) + has_right.astype(jnp.int32))

        @pl.when(has_right)
        def _():
            for h in range(CHUNKS):
                p_copy(0, h).start()

    pl.when(both_near)(open_gate)

    for j in range(SLOTS - 1):
        turned_gap = jnp.where(j < c - 1, jnp.transpose(gap[j]), 0.0)
        for h in range(CHUNKS):
            r = turned_gap[h * W:(h + 1) * W]
            r_in[h, j] = r
            v_in[h, j] = r * (1.0 / CENTRE)
            x_in[h, j] = r * (1.0 / CENTRE)

    rows = lax.broadcasted_iota(jnp.int32, (H, H), 0)

    def selection(pairs):
        sign = jnp.where(pairs > 0, -1.0, 1.0)
        return jnp.where(rows == jnp.abs(pairs) - 1, sign, 0.0).astype(BF16)

    def turned(picked, block):
        high, low = halves(block)
        return nt(picked, high).astype(BF16), nt(picked, low).astype(BF16)

    def left_left(picked, j):
        high, low = turned(picked, ops[j, :H, :H])
        return nt(high, picked), nt(low, picked)

    def left_right(picked, j):
        high, low = halves(jnp.transpose(ops[j, :H, H:]))
        return nt(high, picked).astype(BF16), nt(low, picked).astype(BF16)

    pairs_load.wait()
    pairs = [pairs_ref[j:j + 1, :] for j in range(SLOTS)]
    loads[0].wait()
    picked = selection(pairs[0])
    ll_high, ll_low = left_left(picked, 0)
    ll_out[...] = ll_high + ll_low
    w_ll[0] = ll_high.astype(BF16)
    w_ll[1] = ll_low.astype(BF16)
    w_lr[0], w_lr[1] = left_right(picked, 0)

    for load in loads[1:]:
        load.wait()
    last_pairs = jnp.where(c == 1, pairs[0], jnp.where(c == 2, pairs[1], jnp.where(c == 3, pairs[2], pairs[3])))
    w_p[0, :H], w_p[1, :H] = turned(selection(last_pairs), ops[final_slot, H:, :H])
    w_p[0, H:], w_p[1, H:] = halves(jnp.transpose(ops[final_slot, H:, H:]))

    goes_first = lax.axis_index("grp") % 2 == 0

    @pl.when(jnp.logical_and(both_near, goes_first))
    def _():
        ll_copy.start()

    def product(x, w):
        both = nn(jnp.concatenate(x, axis=0), w[0])
        return (both[:W] + both[W:]) + nn(x[0], w[1])

    def send_p(t, h):
        @pl.when(has_right)
        def _():
            p_copy(t - 1, h).wait_send()

            @pl.when(t < ITERS)
            def _():
                p_copy(t, h).start()

    def end_part(t, h, sends_p=False, guarded=False):
        keep, add = chosen(KEEP, t), chosen(ADD, t)
        partial = p_out[t - 1, h] + far_out[h]
        first = v_in[h, 0]

        @pl.when(jnp.logical_and(has_right, t > 1))
        def _():
            q_copy(t - 1, h).wait_recv()

        r = r_end[h] - jnp.where(has_right, partial + q_got[t - 1, h], 0.0)
        r_end[h] = r

        def rest():
            end = keep * v_end[h] + add * r
            split = halves(end)
            if sends_p:
                p_out[t, h] = pg_out[h] + product(split, (w_p[0, H:], w_p[1, H:]))
                send_p(t, h)
            q_out[t, h] = product(halves(jnp.where(c == 1, end, first)), w_lr)

            @pl.when(has_left)
            def _():
                @pl.when(t > 1)
                def _():
                    q_copy(t - 1, h).wait_send()

                q_copy(t, h).start()

            if not sends_p:
                pl_out[h] = product(split, (w_p[0, H:], w_p[1, H:]))
            v_end[h] = end
            x_end[h] = x_end[h] + end
            far_out[h] = product(split, w_far)
            if guarded:
                heavy_part(t, h, False)

        if guarded:
            pl.when(t <= ITERS)(rest)
        else:
            rest()

    def late_far():
        @pl.when(has_right)
        def _():
            ll_copy.wait_recv()
            w_far[0], w_far[1] = halves(ll_got[...])
            for h in range(CHUNKS):
                far_out[h] = product(halves(v_end[h]), w_far)

    def advance(t, h, j, y):
        r = r_in[h, j] - jnp.where(j < c - 1, y, 0.0)
        v = chosen(KEEP, t + 1) * v_in[h, j] + chosen(ADD, t + 1) * r
        r_in[h, j] = r
        v_in[h, j] = v
        x_in[h, j] = x_in[h, j] + v

    def ghost_part(t, h, sends_p=True, held=False):
        keep, add = chosen(KEEP, t), chosen(ADD, t)
        partial = q_out[t - 1, h] + own[h]
        if held:
            before = before_in[h]
        else:
            before = jnp.where(c == 2, v_in[h, 0], jnp.where(c == 3, v_in[h, 1], v_in[h, 2]))

        @pl.when(has_left)
        def _():
            p_copy(t - 1, h).wait_recv()

        r = r_ghost[h] - jnp.where(has_left, partial + p_got[t - 1, h], 0.0)
        ghost = keep * v_ghost[h] + add * r
        split = halves(ghost)
        from_left = product(halves(jnp.where(c == 1, ghost, before)), (w_p[0, :H], w_p[1, :H]))
        if sends_p:
            p_out[t, h] = from_left + pl_out[h]
        else:
            pg_out[h] = from_left
        y = product(split, (w_in[0, 0, :H], w_in[0, 1, :H]))
        if held:
            advance(t, h, 0, y + row_out[h])
        else:
            row_out[h] = y
        r_ghost[h] = r
        v_ghost[h] = ghost
        if sends_p:
            send_p(t, h)
        own[h] = product(split, w_ll)

    def heavy_part(t, h, finishes):
        inner = [v_in[h, j] for j in range(3)]
        end = v_end[h]
        if not finishes:
            before_in[h] = jnp.where(c == 2, inner[0], jnp.where(c == 3, inner[1], inner[2]))
        blocks = [inner[0]] + [jnp.where(c == j + 1, end, inner[j]) for j in (1, 2)] + [end]
        for i, block in enumerate(blocks):
            high, low = halves(jnp.where(c == 1, end, block) if i == 0 else block)
            vb[h, 0, :, i * H:(i + 1) * H] = high
            vb[h, 1, :, i * H:(i + 1) * H] = low

        def columns(k, width):
            return vb[h, 0, :, k * H:(k + width) * H], vb[h, 1, :, k * H:(k + width) * H]

        y = product(columns(0, 2), (w_in[0, 0, H:], w_in[0, 1, H:]))
        if finishes:
            advance(t, h, 0, y + row_out[h])
        else:
            row_out[h] = y
        for j in (1, 2):
            advance(t, h, j, product(columns(j - 1, 3), w_in.at[j]))

    for j in range(SLOTS):
        picked = selection(pairs[j])
        if j > 0:
            ll_high, ll_low = left_left(picked, j)
            mid_high, mid_low = halves(jnp.transpose(ops[j - 1, H:, H:]) + (ll_high + ll_low))
            w_in[j - 1, 0, H:2 * H] = mid_high
            w_in[j - 1, 1, H:2 * H] = mid_low
            w_in[j - 1, 0, 2 * H:], w_in[j - 1, 1, 2 * H:] = left_right(picked, j)
        if j < SLOTS - 1:
            w_in[j, 0, :H], w_in[j, 1, :H] = turned(picked, ops[j, H:, :H])

    @pl.when(jnp.logical_not(both_near))
    def _():
        open_gate()

        @pl.when(jnp.logical_and(has_left, goes_first))
        def _():
            ll_copy.start()


    @pl.when(left_is_far)
    def _():
        @pl.loop(0, CHUNKS)
        def _(h):
            end_part(1, h)

    def placed(inner, end, j):
        kept = jnp.where(j < c - 1, inner, 0.0) if j < 3 else jnp.zeros_like(end)
        return jnp.transpose(jnp.where(c - 1 == j, end, kept))

    def finish_x():
        end = x_end[...].reshape(RHS, H)
        for j in range(SLOTS):
            out_x[0, 0, j] = placed(x_in[:, j % 3].reshape(RHS, H), end, j)

    def send_later():
        @pl.when(jnp.logical_and(has_left, jnp.logical_not(goes_first)))
        def _():
            ll_copy.start()

    pl.when(jnp.logical_not(left_is_far))(send_later)

    def all_steps(body):
        @pl.loop(0, ITERS * CHUNKS)
        def _(n):
            body(n // CHUNKS + 1, n % CHUNKS, n)

    last = ITERS * CHUNKS - 1

    @pl.when(left_is_far)
    def _():
        @pl.loop(0, CHUNKS)
        def _(h):
            heavy_part(1, h, False)

        send_later()
        late_far()

        @all_steps
        def _(t, h, n):
            pl.when(n == last)(finish_x)
            ghost_part(t, h, held=True)
            end_part(t + 1, h, guarded=True)

    @pl.when(right_is_far)
    def _():
        @all_steps
        def _(t, h, n):
            ghost_part(t, h, sends_p=False)
            end_part(t, h, sends_p=True)
            heavy_part(t, h, True)
            pl.when(n == CHUNKS - 1)(late_far)
            pl.when(n == last)(finish_x)

    @pl.when(both_near)
    def _():
        @all_steps
        def _(t, h, n):
            end_part(t, h)
            pl.when(n == last)(finish_x)
            ghost_part(t, h)
            heavy_part(t, h, True)
            pl.when(n == CHUNKS - 1)(late_far)

    end = jnp.zeros((RHS, H), F32)
    for j in range(SLOTS):
        out_r[0, 0, j] = placed(r_in[:, j % 3].reshape(RHS, H), end, j)

    @pl.when(jnp.logical_and(jnp.logical_not(left_is_far), has_right))
    def _():
        @pl.loop(0, CHUNKS)
        def _(h):
            q_copy(ITERS, h).wait_recv()
            r_end[h] = r_end[h] - (p_out[ITERS, h] + far_out[h] + q_got[ITERS, h])

    end = jnp.transpose(r_end[...].reshape(RHS, H))
    for j in range(SLOTS):
        out_r[0, 0, j] = jnp.where(c - 1 == j, end, out_r[0, 0, j])

    @pl.when(has_left)
    def _():
        ll_copy.wait_send()
        for h in range(CHUNKS):
            q_copy(ITERS, h).wait_send()


def put_out(x, r, out_x, out_r, sems):
    stores = [pltpu.make_async_copy(x, out_x, sems.at[0]), pltpu.make_async_copy(r, out_r, sems.at[1])]
    for store in stores:
        store.start()
    for store in stores:
        store.wait()


def shards(far, operators, counts, pair_rows, gap):
    hbm = pl.BlockSpec(memory_space=pltpu.HBM)
    vmem = pl.BlockSpec(memory_space=pltpu.VMEM)
    dma = pltpu.SemaphoreType.DMA
    message = pltpu.VMEM((ITERS + 1, CHUNKS, W, H), F32)
    chunk = pltpu.VMEM((CHUNKS, W, H), F32)
    inner = pltpu.VMEM((CHUNKS, 3, W, H), F32)
    operator = pltpu.VMEM((2, H, H), BF16)
    block = jax.ShapeDtypeStruct((1, 1, SLOTS, H, RHS), F32)
    results = pl.pallas_call(
        functools.partial(kernel, far),
        out_shape=(block, block),
        in_specs=[pl.BlockSpec(memory_space=pltpu.SMEM), hbm, hbm, hbm],
        out_specs=(vmem, vmem),
        scratch_shapes=[
            pltpu.VMEM((SLOTS, M, M), F32),
            pltpu.VMEM((SLOTS, H, RHS), F32),
            pltpu.VMEM((SLOTS, H), jnp.int32),
            pltpu.VMEM((3, 2, 3 * H, H), BF16),
            pltpu.VMEM((2, 2 * H, H), BF16),
            operator,
            operator,
            operator,
            pltpu.VMEM((CHUNKS, 2, W, 4 * H), BF16),
            chunk, chunk, chunk, chunk, chunk, chunk, chunk, chunk, chunk, chunk,
            inner, inner, inner,
            chunk,
            message, message, message, message,
            pltpu.VMEM((H, H), F32),
            pltpu.VMEM((H, H), F32),
            dma((SLOTS,)),
            dma((2,)),
            dma((2,)),
            dma((CHUNKS,)),
            dma((ITERS + 1, CHUNKS)),
            dma((CHUNKS,)),
            dma((ITERS + 1, CHUNKS)),
        ],
        compiler_params=pltpu.CompilerParams(
            collective_id=0, has_side_effects=True, vmem_limit_bytes=55_200_000),
        name="feti_chebyshev",
    )(counts, pltpu.with_memory_space_constraint(pair_rows, pltpu.HBM), operators, gap)
    return pl.pallas_call(
        put_out,
        out_shape=(block, block),
        in_specs=[vmem, vmem],
        out_specs=(hbm, hbm),
        scratch_shapes=[dma((2,))],
        compiler_params=pltpu.CompilerParams(vmem_limit_bytes=8 * 1024 * 1024),
        name="put_out",
    )(*results)


def solution(mesh):
    return jax.shard_map(
        functools.partial(shards, 16 if mesh.shape["sub"] % 16 == 0 else 2),
        mesh=mesh,
        in_specs=(
            P("grp", "sub", None, None, None),
            P("grp", "sub"),
            P("grp", "sub", None, None),
            P("grp", "sub", None, None, None),
        ),
        out_specs=(P("grp", "sub", None, None, None), P("grp", "sub", None, None, None)),
        check_vma=False,
    )
```

```python
import functools

import jax
import jax.numpy as jnp
from jax import lax
from jax.experimental import pallas as pl
from jax.experimental.pallas import tpu as pltpu
from jax.sharding import PartitionSpec as P

M = 512
H = 256
RHS = 128
SLOTS = 4
ITERS = 6
CHUNKS = 2
W = RHS // CHUNKS
PAIR = 2
PAIRS = CHUNKS // PAIR

LOWER = 1.0
UPPER = 14.0
CENTRE = (UPPER + LOWER) / 2.0
RADIUS = (UPPER - LOWER) / 2.0

F32 = jnp.float32
BF16 = jnp.bfloat16


def coefficients():
    spread = CENTRE / RADIUS
    rho = 1.0 / spread
    keep, add = {1: 0.0}, {1: 1.0 / CENTRE}
    for t in range(2, ITERS + 1):
        new = 1.0 / (2.0 * spread - rho)
        keep[t] = new * rho
        add[t] = 2.0 * new / RADIUS
        rho = new
    keep[ITERS + 1] = add[ITERS + 1] = 0.0
    return keep, add


KEEP, ADD = coefficients()


def chosen(table, t):
    value = jnp.float32(table[ITERS + 1])
    for k in range(1, ITERS + 1):
        value = jnp.where(t == k, jnp.float32(table[k]), value)
    return value


def halves(x):
    high = x.astype(BF16)
    low = (x - high.astype(F32)).astype(BF16)
    return high, low


def nn(a, b):
    return jnp.dot(a, b, preferred_element_type=F32)


def nt(a, b):
    return lax.dot_general(a, b, (((1,), (1,)), ((), ())), preferred_element_type=F32)


def kernel(far, cnt_ref, pairs_hbm, ops_hbm, gap_hbm, out_x, out_r,
           ops, gap, pairs_ref, w_in, w_p, w_ll, w_lr, w_far, vb, far_out, pg_out, pl_out, row_out, before_in, v_ghost, r_ghost, v_end, r_end, x_end, v_in, r_in, x_in, own,
           p_out, p_got, q_out, q_got, ll_out, ll_got,
           load_sem, gap_sem, ll_sem, p_send, p_recv, q_send, q_recv):
    s = lax.axis_index("sub")
    has_left = s > 0
    has_right = s < lax.axis_size("sub") - 1
    left_is_far = s % far == 0
    right_is_far = s % far == far - 1
    both_near = jnp.logical_not(jnp.logical_or(left_is_far, right_is_far))
    c = cnt_ref[0, 0]
    final_slot = jnp.clip(c - 1, 0, SLOTS - 1)

    barrier = pltpu.get_barrier_semaphore()

    @pl.when(has_left)
    def _():
        pl.semaphore_signal(barrier, inc=1, device_id={"sub": s - 1}, device_id_type=pl.DeviceIdType.MESH)

    @pl.when(has_right)
    def _():
        pl.semaphore_signal(barrier, inc=1, device_id={"sub": s + 1}, device_id_type=pl.DeviceIdType.MESH)

    pairs_load = pltpu.make_async_copy(pairs_hbm.at[0, 0], pairs_ref, gap_sem.at[1])
    pairs_load.start()
    gap_load = pltpu.make_async_copy(gap_hbm.at[0, 0], gap, gap_sem.at[0])
    gap_load.start()
    loads = [pltpu.make_async_copy(ops_hbm.at[0, 0, j], ops.at[j], load_sem.at[j]) for j in range(SLOTS)]
    for load in loads:
        load.start()

    @pl.when(jnp.logical_not(has_left))
    def _():
        p_got[...] = jnp.zeros_like(p_got)

    @pl.when(jnp.logical_not(has_right))
    def _():
        q_got[...] = jnp.zeros_like(q_got)

    for ref in (v_ghost, r_ghost, v_end, r_end, x_end, own, far_out, w_far):
        ref[...] = jnp.zeros_like(ref)
    q_out[0] = jnp.zeros(q_out.shape[1:], F32)
    q_got[0] = jnp.zeros(q_got.shape[1:], F32)

    def p_copy(t, h):
        return pltpu.make_async_remote_copy(
            src_ref=p_out.at[t, h], dst_ref=p_got.at[t, h], send_sem=p_send.at[h], recv_sem=p_recv.at[t, h],
            device_id={"sub": s + 1}, device_id_type=pl.DeviceIdType.MESH)

    def q_copy(t, h):
        return pltpu.make_async_remote_copy(
            src_ref=q_out.at[t, h], dst_ref=q_got.at[t, h], send_sem=q_send.at[h], recv_sem=q_recv.at[t, h],
            device_id={"sub": s - 1}, device_id_type=pl.DeviceIdType.MESH)

    ll_copy = pltpu.make_async_remote_copy(
        src_ref=ll_out, dst_ref=ll_got, send_sem=ll_sem.at[0], recv_sem=ll_sem.at[1],
        device_id={"sub": s - 1}, device_id_type=pl.DeviceIdType.MESH)

    gap_load.wait()
    top = jnp.where(has_right, jnp.transpose(gap[final_slot]), 0.0)
    for h in range(CHUNKS):
        p_out[0, h] = -top[h * W:(h + 1) * W]

    def open_gate():
        pl.semaphore_wait(barrier, has_left.astype(jnp.int32) + has_right.astype(jnp.int32))

        @pl.when(has_right)
        def _():
            for h in range(CHUNKS):
                p_copy(0, h).start()

    pl.when(both_near)(open_gate)

    for j in range(SLOTS - 1):
        turned_gap = jnp.where(j < c - 1, jnp.transpose(gap[j]), 0.0)
        for h in range(CHUNKS):
            r = turned_gap[h * W:(h + 1) * W]
            r_in[h, j] = r
            v_in[h, j] = r * (1.0 / CENTRE)
            x_in[h, j] = r * (1.0 / CENTRE)

    rows = lax.broadcasted_iota(jnp.int32, (H, H), 0)

    def selection(pairs):
        sign = jnp.where(pairs > 0, -1.0, 1.0)
        return jnp.where(rows == jnp.abs(pairs) - 1, sign, 0.0).astype(BF16)

    def turned(picked, block):
        high, low = halves(block)
        return nt(picked, high).astype(BF16), nt(picked, low).astype(BF16)

    def left_left(picked, j):
        high, low = turned(picked, ops[j, :H, :H])
        return nt(high, picked), nt(low, picked)

    def left_right(picked, j):
        high, low = halves(jnp.transpose(ops[j, :H, H:]))
        return nt(high, picked).astype(BF16), nt(low, picked).astype(BF16)

    pairs_load.wait()
    pairs = [pairs_ref[j:j + 1, :] for j in range(SLOTS)]
    loads[0].wait()
    picked = selection(pairs[0])
    ll_high, ll_low = left_left(picked, 0)
    ll_out[...] = ll_high + ll_low
    w_ll[0] = ll_high.astype(BF16)
    w_ll[1] = ll_low.astype(BF16)
    w_lr[0], w_lr[1] = left_right(picked, 0)

    for load in loads[1:]:
        load.wait()
    last_pairs = jnp.where(c == 1, pairs[0], jnp.where(c == 2, pairs[1], jnp.where(c == 3, pairs[2], pairs[3])))
    w_p[0, :H], w_p[1, :H] = turned(selection(last_pairs), ops[final_slot, H:, :H])
    w_p[0, H:], w_p[1, H:] = halves(jnp.transpose(ops[final_slot, H:, H:]))

    goes_first = lax.axis_index("grp") % 2 == 0

    def product(x, w):
        both = nn(jnp.concatenate(x, axis=0), w[0])
        width = both.shape[0] // 2
        return (both[:width] + both[width:]) + nn(x[0], w[1])

    def paired(g):
        return pl.ds(g * PAIR, PAIR)

    def joined(x):
        return x.reshape(x.shape[0] * W, H)

    def send_p(t, h):
        @pl.when(has_right)
        def _():
            p_copy(t - 1, h).wait_send()

            @pl.when(t < ITERS)
            def _():
                p_copy(t, h).start()

    def end_part(t, h, sends_p=False, guarded=False):
        keep, add = chosen(KEEP, t), chosen(ADD, t)
        partial = p_out[t - 1, h] + far_out[h]
        first = v_in[h, 0]

        @pl.when(jnp.logical_and(has_right, t > 1))
        def _():
            q_copy(t - 1, h).wait_recv()

        r = r_end[h] - jnp.where(has_right, partial + q_got[t - 1, h], 0.0)
        r_end[h] = r

        def rest():
            end = keep * v_end[h] + add * r
            split = halves(end)
            if sends_p:
                p_out[t, h] = pg_out[h] + product(split, (w_p[0, H:], w_p[1, H:]))
                send_p(t, h)
            q_out[t, h] = product(halves(jnp.where(c == 1, end, first)), w_lr)

            @pl.when(has_left)
            def _():
                @pl.when(t > 1)
                def _():
                    q_copy(t - 1, h).wait_send()

                q_copy(t, h).start()

            if not sends_p:
                pl_out[h] = product(split, (w_p[0, H:], w_p[1, H:]))
            v_end[h] = end
            x_end[h] = x_end[h] + end
            far_out[h] = product(split, w_far)
        if guarded:
            pl.when(t <= ITERS)(rest)
        else:
            rest()

    def late_far():
        @pl.when(has_right)
        def _():
            ll_copy.wait_recv()
            w_far[0], w_far[1] = halves(ll_got[...])
            for h in range(CHUNKS):
                far_out[h] = product(halves(v_end[h]), w_far)

    def advance(t, h, j, y):
        r = r_in[h, j] - jnp.where(j < c - 1, y, 0.0)
        v = chosen(KEEP, t + 1) * v_in[h, j] + chosen(ADD, t + 1) * r
        r_in[h, j] = r
        v_in[h, j] = v
        x_in[h, j] = x_in[h, j] + v

    def ghost_part(t, h, sends_p=True, held=False):
        keep, add = chosen(KEEP, t), chosen(ADD, t)
        partial = q_out[t - 1, h] + own[h]
        if held:
            before = before_in[h]
        else:
            before = jnp.where(c == 2, v_in[h, 0], jnp.where(c == 3, v_in[h, 1], v_in[h, 2]))

        @pl.when(has_left)
        def _():
            p_copy(t - 1, h).wait_recv()

        r = r_ghost[h] - jnp.where(has_left, partial + p_got[t - 1, h], 0.0)
        ghost = keep * v_ghost[h] + add * r
        split = halves(ghost)
        from_left = product(halves(jnp.where(c == 1, ghost, before)), (w_p[0, :H], w_p[1, :H]))
        if sends_p:
            p_out[t, h] = from_left + pl_out[h]
        else:
            pg_out[h] = from_left
        y = product(split, (w_in[0, 0, :H], w_in[0, 1, :H]))
        if held:
            advance(t, h, 0, y + row_out[h])
        else:
            row_out[h] = y
        r_ghost[h] = r
        v_ghost[h] = ghost
        if sends_p:
            send_p(t, h)
        own[h] = product(split, w_ll)

    def advance_pair(t, g, j, y):
        at = paired(g)
        r = joined(r_in[at, j]) - jnp.where(j < c - 1, y, 0.0)
        v = chosen(KEEP, t + 1) * joined(v_in[at, j]) + chosen(ADD, t + 1) * r
        x = joined(x_in[at, j]) + v
        r_in[at, j] = r.reshape(PAIR, W, H)
        v_in[at, j] = v.reshape(PAIR, W, H)
        x_in[at, j] = x.reshape(PAIR, W, H)

    def heavy_part(t, g, finishes):
        at = paired(g)
        inner = [joined(v_in[at, j]) for j in range(3)]
        end = joined(v_end[at])
        if not finishes:
            before = jnp.where(c == 2, inner[0], jnp.where(c == 3, inner[1], inner[2]))
            before_in[at] = before.reshape(PAIR, W, H)
        blocks = [jnp.where(c == j + 1, end, inner[j]) for j in range(3)] + [end]
        for i, block in enumerate(blocks):
            high, low = halves(block)
            vb[0, :, i * H:(i + 1) * H] = high
            vb[1, :, i * H:(i + 1) * H] = low

        def columns(k, width):
            return vb[0, :, k * H:(k + width) * H], vb[1, :, k * H:(k + width) * H]

        y = product(columns(0, 2), (w_in[0, 0, H:], w_in[0, 1, H:]))
        if finishes:
            advance_pair(t, g, 0, y + joined(row_out[at]))
        else:
            row_out[at] = y.reshape(PAIR, W, H)
        for j in (1, 2):
            advance_pair(t, g, j, product(columns(j - 1, 3), w_in.at[j]))

    for j in range(SLOTS):
        picked = selection(pairs[j])
        if j > 0:
            ll_high, ll_low = left_left(picked, j)
            mid_high, mid_low = halves(jnp.transpose(ops[j - 1, H:, H:]) + (ll_high + ll_low))
            w_in[j - 1, 0, H:2 * H] = mid_high
            w_in[j - 1, 1, H:2 * H] = mid_low
            w_in[j - 1, 0, 2 * H:], w_in[j - 1, 1, 2 * H:] = left_right(picked, j)
        if j < SLOTS - 1:
            w_in[j, 0, :H], w_in[j, 1, :H] = turned(picked, ops[j, H:, :H])

    @pl.when(jnp.logical_not(both_near))
    def _():
        open_gate()

        @pl.when(jnp.logical_and(has_left, goes_first))
        def _():
            ll_copy.start()


    @pl.when(left_is_far)
    def _():
        @pl.loop(0, CHUNKS)
        def _(h):
            end_part(1, h)

    def placed(inner, end, j):
        kept = jnp.where(j < c - 1, inner, 0.0) if j < 3 else jnp.zeros_like(end)
        return jnp.transpose(jnp.where(c - 1 == j, end, kept))

    def finish_x():
        end = x_end[...].reshape(RHS, H)
        for j in range(SLOTS):
            out_x[0, 0, j] = placed(x_in[:, j % 3].reshape(RHS, H), end, j)

    def send_later():
        @pl.when(jnp.logical_and(has_left, jnp.logical_or(both_near, jnp.logical_not(goes_first))))
        def _():
            ll_copy.start()

    pl.when(jnp.logical_not(left_is_far))(send_later)

    def all_steps(body):
        @pl.loop(0, ITERS * PAIRS)
        def _(n):
            t, g = n // PAIRS + 1, n % PAIRS
            body(t, g, [g * PAIR + k for k in range(PAIR)], n)

    last = ITERS * PAIRS - 1

    @pl.when(left_is_far)
    def _():
        @pl.loop(0, PAIRS)
        def _(g):
            heavy_part(1, g, False)

        send_later()
        late_far()

        @all_steps
        def _(t, g, chunks, n):
            pl.when(n == last)(finish_x)
            for h in chunks:
                ghost_part(t, h, held=True)
                end_part(t + 1, h, guarded=True)
            pl.when(t < ITERS)(lambda: heavy_part(t + 1, g, False))

    @pl.when(right_is_far)
    def _():
        @all_steps
        def _(t, g, chunks, n):
            for k, h in enumerate(chunks):
                ghost_part(t, h, sends_p=False)
                if k == 0:
                    pl.when(n == PAIRS)(late_far)
                end_part(t, h, sends_p=True)
            heavy_part(t, g, True)
            pl.when(n == last)(finish_x)

    @pl.when(both_near)
    def _():
        @all_steps
        def _(t, g, chunks, n):
            for k, h in enumerate(chunks):
                end_part(t, h)
                if k == PAIR - 1:
                    pl.when(n == last)(finish_x)
                ghost_part(t, h)
            heavy_part(t, g, True)
            pl.when(n == PAIRS - 1)(late_far)

    end = jnp.zeros((RHS, H), F32)
    for j in range(SLOTS):
        out_r[0, 0, j] = placed(r_in[:, j % 3].reshape(RHS, H), end, j)

    @pl.when(jnp.logical_and(jnp.logical_not(left_is_far), has_right))
    def _():
        @pl.loop(0, CHUNKS)
        def _(h):
            q_copy(ITERS, h).wait_recv()
            r_end[h] = r_end[h] - (p_out[ITERS, h] + far_out[h] + q_got[ITERS, h])

    end = jnp.transpose(r_end[...].reshape(RHS, H))
    for j in range(SLOTS):
        out_r[0, 0, j] = jnp.where(c - 1 == j, end, out_r[0, 0, j])

    @pl.when(has_left)
    def _():
        ll_copy.wait_send()
        for h in range(CHUNKS):
            q_copy(ITERS, h).wait_send()


def put_out(x, r, out_x, out_r, sems):
    stores = [pltpu.make_async_copy(x, out_x, sems.at[0]), pltpu.make_async_copy(r, out_r, sems.at[1])]
    for store in stores:
        store.start()
    for store in stores:
        store.wait()


def shards(far, operators, counts, pair_rows, gap):
    hbm = pl.BlockSpec(memory_space=pltpu.HBM)
    vmem = pl.BlockSpec(memory_space=pltpu.VMEM)
    dma = pltpu.SemaphoreType.DMA
    message = pltpu.VMEM((ITERS + 1, CHUNKS, W, H), F32)
    chunk = pltpu.VMEM((CHUNKS, W, H), F32)
    inner = pltpu.VMEM((CHUNKS, 3, W, H), F32)
    operator = pltpu.VMEM((2, H, H), BF16)
    block = jax.ShapeDtypeStruct((1, 1, SLOTS, H, RHS), F32)
    results = pl.pallas_call(
        functools.partial(kernel, far),
        out_shape=(block, block),
        in_specs=[pl.BlockSpec(memory_space=pltpu.SMEM), hbm, hbm, hbm],
        out_specs=(vmem, vmem),
        scratch_shapes=[
            pltpu.VMEM((SLOTS, M, M), F32),
            pltpu.VMEM((SLOTS, H, RHS), F32),
            pltpu.VMEM((SLOTS, H), jnp.int32),
            pltpu.VMEM((3, 2, 3 * H, H), BF16),
            pltpu.VMEM((2, 2 * H, H), BF16),
            operator,
            operator,
            operator,
            pltpu.VMEM((2, PAIR * W, 4 * H), BF16),
            chunk, chunk, chunk, chunk, chunk, chunk, chunk, chunk, chunk, chunk,
            inner, inner, inner,
            chunk,
            message, message, message, message,
            pltpu.VMEM((H, H), F32),
            pltpu.VMEM((H, H), F32),
            dma((SLOTS,)),
            dma((2,)),
            dma((2,)),
            dma((CHUNKS,)),
            dma((ITERS + 1, CHUNKS)),
            dma((CHUNKS,)),
            dma((ITERS + 1, CHUNKS)),
        ],
        compiler_params=pltpu.CompilerParams(
            collective_id=0, has_side_effects=True, vmem_limit_bytes=55_200_000),
        name="feti_chebyshev",
    )(counts, pltpu.with_memory_space_constraint(pair_rows, pltpu.HBM), operators, gap)
    return pl.pallas_call(
        put_out,
        out_shape=(block, block),
        in_specs=[vmem, vmem],
        out_specs=(hbm, hbm),
        scratch_shapes=[dma((2,))],
        compiler_params=pltpu.CompilerParams(vmem_limit_bytes=8 * 1024 * 1024),
        name="put_out",
    )(*results)


def solution(mesh):
    return jax.shard_map(
        functools.partial(shards, 16 if mesh.shape["sub"] % 16 == 0 else 2),
        mesh=mesh,
        in_specs=(
            P("grp", "sub", None, None, None),
            P("grp", "sub"),
            P("grp", "sub", None, None),
            P("grp", "sub", None, None, None),
        ),
        out_specs=(P("grp", "sub", None, None, None), P("grp", "sub", None, None, None)),
        check_vma=False,
    )
```

```python
import functools

import jax
import jax.numpy as jnp
from jax import lax
from jax.experimental import pallas as pl
from jax.experimental.pallas import tpu as pltpu
from jax.sharding import PartitionSpec as P

M = 512
H = 256
RHS = 128
SLOTS = 4
ITERS = 6
CHUNKS = 2
W = RHS // CHUNKS
PAIR = 2
PAIRS = CHUNKS // PAIR

LOWER = 1.0
UPPER = 14.0
CENTRE = (UPPER + LOWER) / 2.0
RADIUS = (UPPER - LOWER) / 2.0

F32 = jnp.float32
BF16 = jnp.bfloat16


def coefficients():
    spread = CENTRE / RADIUS
    rho = 1.0 / spread
    keep, add = {1: 0.0}, {1: 1.0 / CENTRE}
    for t in range(2, ITERS + 1):
        new = 1.0 / (2.0 * spread - rho)
        keep[t] = new * rho
        add[t] = 2.0 * new / RADIUS
        rho = new
    keep[ITERS + 1] = add[ITERS + 1] = 0.0
    return keep, add


KEEP, ADD = coefficients()


def chosen(table, t):
    value = jnp.float32(table[ITERS + 1])
    for k in range(1, ITERS + 1):
        value = jnp.where(t == k, jnp.float32(table[k]), value)
    return value


def halves(x):
    high = x.astype(BF16)
    low = (x - high.astype(F32)).astype(BF16)
    return high, low


def nn(a, b):
    return jnp.dot(a, b, preferred_element_type=F32)


def nt(a, b):
    return lax.dot_general(a, b, (((1,), (1,)), ((), ())), preferred_element_type=F32)


def kernel(far, cnt_ref, pairs_hbm, ops_hbm, gap_hbm, out_x, out_r,
           ops, gap, pairs_ref, w_in, w_p, w_ll, w_lr, w_far, vb, far_out, pg_out, pl_out, row_out, before_in, v_ghost, r_ghost, v_end, r_end, x_end, v_in, r_in, x_in, own,
           p_out, p_got, q_out, q_got, ll_out, ll_got,
           load_sem, gap_sem, ll_sem, p_send, p_recv, q_send, q_recv):
    s = lax.axis_index("sub")
    has_left = s > 0
    has_right = s < lax.axis_size("sub") - 1
    left_is_far = s % far == 0
    right_is_far = s % far == far - 1
    both_near = jnp.logical_not(jnp.logical_or(left_is_far, right_is_far))
    c = cnt_ref[0, 0]
    final_slot = jnp.clip(c - 1, 0, SLOTS - 1)

    barrier = pltpu.get_barrier_semaphore()

    @pl.when(has_left)
    def _():
        pl.semaphore_signal(barrier, inc=1, device_id={"sub": s - 1}, device_id_type=pl.DeviceIdType.MESH)

    @pl.when(has_right)
    def _():
        pl.semaphore_signal(barrier, inc=1, device_id={"sub": s + 1}, device_id_type=pl.DeviceIdType.MESH)

    pairs_load = pltpu.make_async_copy(pairs_hbm.at[0, 0], pairs_ref, gap_sem.at[1])
    pairs_load.start()
    gap_load = pltpu.make_async_copy(gap_hbm.at[0, 0], gap, gap_sem.at[0])
    gap_load.start()
    loads = [pltpu.make_async_copy(ops_hbm.at[0, 0, j], ops.at[j], load_sem.at[j]) for j in range(SLOTS)]
    for load in loads:
        load.start()

    @pl.when(jnp.logical_not(has_left))
    def _():
        p_got[...] = jnp.zeros_like(p_got)

    @pl.when(jnp.logical_not(has_right))
    def _():
        q_got[...] = jnp.zeros_like(q_got)

    for ref in (v_ghost, r_ghost, v_end, r_end, x_end, own, far_out, w_far):
        ref[...] = jnp.zeros_like(ref)
    q_out[0] = jnp.zeros(q_out.shape[1:], F32)
    q_got[0] = jnp.zeros(q_got.shape[1:], F32)

    def p_copy(t, h):
        return pltpu.make_async_remote_copy(
            src_ref=p_out.at[t, h], dst_ref=p_got.at[t, h], send_sem=p_send.at[h], recv_sem=p_recv.at[t, h],
            device_id={"sub": s + 1}, device_id_type=pl.DeviceIdType.MESH)

    def q_copy(t, h):
        return pltpu.make_async_remote_copy(
            src_ref=q_out.at[t, h], dst_ref=q_got.at[t, h], send_sem=q_send.at[h], recv_sem=q_recv.at[t, h],
            device_id={"sub": s - 1}, device_id_type=pl.DeviceIdType.MESH)

    ll_copy = pltpu.make_async_remote_copy(
        src_ref=ll_out, dst_ref=ll_got, send_sem=ll_sem.at[0], recv_sem=ll_sem.at[1],
        device_id={"sub": s - 1}, device_id_type=pl.DeviceIdType.MESH)

    gap_load.wait()
    top = jnp.where(has_right, jnp.transpose(gap[final_slot]), 0.0)
    for h in range(CHUNKS):
        p_out[0, h] = -top[h * W:(h + 1) * W]

    def open_gate():
        pl.semaphore_wait(barrier, has_left.astype(jnp.int32) + has_right.astype(jnp.int32))

        @pl.when(has_right)
        def _():
            for h in range(CHUNKS):
                p_copy(0, h).start()

    pl.when(both_near)(open_gate)

    for j in range(SLOTS - 1):
        turned_gap = jnp.where(j < c - 1, jnp.transpose(gap[j]), 0.0)
        for h in range(CHUNKS):
            r = turned_gap[h * W:(h + 1) * W]
            r_in[h, j] = r
            v_in[h, j] = r * (1.0 / CENTRE)
            x_in[h, j] = r * (1.0 / CENTRE)

    rows = lax.broadcasted_iota(jnp.int32, (H, H), 0)

    def selection(pairs):
        sign = jnp.where(pairs > 0, -1.0, 1.0)
        return jnp.where(rows == jnp.abs(pairs) - 1, sign, 0.0).astype(BF16)

    def turned(picked, block):
        high, low = halves(block)
        return nt(picked, high).astype(BF16), nt(picked, low).astype(BF16)

    def left_left(picked, j):
        high, low = turned(picked, ops[j, :H, :H])
        return nt(high, picked), nt(low, picked)

    def left_right(picked, j):
        high, low = halves(jnp.transpose(ops[j, :H, H:]))
        return nt(high, picked).astype(BF16), nt(low, picked).astype(BF16)

    pairs_load.wait()
    pairs = [pairs_ref[j:j + 1, :] for j in range(SLOTS)]
    loads[0].wait()
    picked = selection(pairs[0])
    ll_high, ll_low = left_left(picked, 0)
    ll_out[...] = ll_high + ll_low
    w_ll[0] = ll_high.astype(BF16)
    w_ll[1] = ll_low.astype(BF16)
    w_lr[0], w_lr[1] = left_right(picked, 0)

    for load in loads[1:]:
        load.wait()
    last_pairs = jnp.where(c == 1, pairs[0], jnp.where(c == 2, pairs[1], jnp.where(c == 3, pairs[2], pairs[3])))
    w_p[0, :H], w_p[1, :H] = turned(selection(last_pairs), ops[final_slot, H:, :H])
    w_p[0, H:], w_p[1, H:] = halves(jnp.transpose(ops[final_slot, H:, H:]))

    goes_first = lax.axis_index("grp") % 2 == 0

    def product(x, w):
        both = nn(jnp.concatenate(x, axis=0), w[0])
        width = both.shape[0] // 2
        return (both[:width] + both[width:]) + nn(x[0], w[1])

    def paired(g):
        return pl.ds(g * PAIR, PAIR)

    def joined(x):
        return x.reshape(x.shape[0] * W, H)

    def send_p(t, h):
        @pl.when(has_right)
        def _():
            p_copy(t - 1, h).wait_send()

            @pl.when(t < ITERS)
            def _():
                p_copy(t, h).start()

    def end_part(t, h, sends_p=False, guarded=False):
        keep, add = chosen(KEEP, t), chosen(ADD, t)
        partial = p_out[t - 1, h] + far_out[h]
        first = v_in[h, 0]

        @pl.when(jnp.logical_and(has_right, t > 1))
        def _():
            q_copy(t - 1, h).wait_recv()

        r = r_end[h] - jnp.where(has_right, partial + q_got[t - 1, h], 0.0)
        r_end[h] = r

        def rest():
            end = keep * v_end[h] + add * r
            split = halves(end)
            if sends_p:
                p_out[t, h] = pg_out[h] + product(split, (w_p[0, H:], w_p[1, H:]))
                send_p(t, h)
            q_out[t, h] = product(halves(jnp.where(c == 1, end, first)), w_lr)

            @pl.when(has_left)
            def _():
                @pl.when(t > 1)
                def _():
                    q_copy(t - 1, h).wait_send()

                q_copy(t, h).start()

            if not sends_p:
                pl_out[h] = product(split, (w_p[0, H:], w_p[1, H:]))
            v_end[h] = end
            x_end[h] = x_end[h] + end
            far_out[h] = product(split, w_far)
        if guarded:
            pl.when(t <= ITERS)(rest)
        else:
            rest()

    def late_far():
        @pl.when(has_right)
        def _():
            ll_copy.wait_recv()
            w_far[0], w_far[1] = halves(ll_got[...])
            for h in range(CHUNKS):
                far_out[h] = product(halves(v_end[h]), w_far)

    def advance(t, h, j, y):
        r = r_in[h, j] - jnp.where(j < c - 1, y, 0.0)
        v = chosen(KEEP, t + 1) * v_in[h, j] + chosen(ADD, t + 1) * r
        r_in[h, j] = r
        v_in[h, j] = v
        x_in[h, j] = x_in[h, j] + v

    def ghost_part(t, h, sends_p=True, held=False):
        keep, add = chosen(KEEP, t), chosen(ADD, t)
        partial = q_out[t - 1, h] + own[h]
        if held:
            before = before_in[h]
        else:
            before = jnp.where(c == 2, v_in[h, 0], jnp.where(c == 3, v_in[h, 1], v_in[h, 2]))

        @pl.when(has_left)
        def _():
            p_copy(t - 1, h).wait_recv()

        r = r_ghost[h] - jnp.where(has_left, partial + p_got[t - 1, h], 0.0)
        ghost = keep * v_ghost[h] + add * r
        split = halves(ghost)
        from_left = product(halves(jnp.where(c == 1, ghost, before)), (w_p[0, :H], w_p[1, :H]))
        if sends_p:
            p_out[t, h] = from_left + pl_out[h]
        else:
            pg_out[h] = from_left
        y = product(split, (w_in[0, 0, :H], w_in[0, 1, :H]))
        if held:
            advance(t, h, 0, y + row_out[h])
        else:
            row_out[h] = y
        r_ghost[h] = r
        v_ghost[h] = ghost
        if sends_p:
            send_p(t, h)
        own[h] = product(split, w_ll)

    def advance_pair(t, g, j, y):
        at = paired(g)
        r = joined(r_in[at, j]) - jnp.where(j < c - 1, y, 0.0)
        v = chosen(KEEP, t + 1) * joined(v_in[at, j]) + chosen(ADD, t + 1) * r
        x = joined(x_in[at, j]) + v
        r_in[at, j] = r.reshape(PAIR, W, H)
        v_in[at, j] = v.reshape(PAIR, W, H)
        x_in[at, j] = x.reshape(PAIR, W, H)

    def heavy_part(t, g, finishes):
        at = paired(g)
        inner = [joined(v_in[at, j]) for j in range(3)]
        end = joined(v_end[at])
        if not finishes:
            before = jnp.where(c == 2, inner[0], jnp.where(c == 3, inner[1], inner[2]))
            before_in[at] = before.reshape(PAIR, W, H)
        blocks = [jnp.where(c == j + 1, end, inner[j]) for j in range(3)] + [end]
        for i, block in enumerate(blocks):
            high, low = halves(block)
            vb[0, :, i * H:(i + 1) * H] = high
            vb[1, :, i * H:(i + 1) * H] = low

        def columns(k, width):
            return vb[0, :, k * H:(k + width) * H], vb[1, :, k * H:(k + width) * H]

        y = product(columns(0, 2), (w_in[0, 0, H:], w_in[0, 1, H:]))
        if finishes:
            advance_pair(t, g, 0, y + joined(row_out[at]))
        else:
            row_out[at] = y.reshape(PAIR, W, H)
        for j in (1, 2):
            advance_pair(t, g, j, product(columns(j - 1, 3), w_in.at[j]))

    for j in range(SLOTS):
        picked = selection(pairs[j])
        if j > 0:
            ll_high, ll_low = left_left(picked, j)
            mid_high, mid_low = halves(jnp.transpose(ops[j - 1, H:, H:]) + (ll_high + ll_low))
            w_in[j - 1, 0, H:2 * H] = mid_high
            w_in[j - 1, 1, H:2 * H] = mid_low
            w_in[j - 1, 0, 2 * H:], w_in[j - 1, 1, 2 * H:] = left_right(picked, j)
        if j < SLOTS - 1:
            w_in[j, 0, :H], w_in[j, 1, :H] = turned(picked, ops[j, H:, :H])

    @pl.when(jnp.logical_not(both_near))
    def _():
        open_gate()

        @pl.when(jnp.logical_and(has_left, goes_first))
        def _():
            ll_copy.start()


    @pl.when(left_is_far)
    def _():
        @pl.loop(0, CHUNKS)
        def _(h):
            end_part(1, h)

    def placed(inner, end, j):
        kept = jnp.where(j < c - 1, inner, 0.0) if j < 3 else jnp.zeros_like(end)
        return jnp.transpose(jnp.where(c - 1 == j, end, kept))

    def finish_x():
        end = x_end[...].reshape(RHS, H)
        for j in range(SLOTS):
            out_x[0, 0, j] = placed(x_in[:, j % 3].reshape(RHS, H), end, j)

    def send_later():
        @pl.when(jnp.logical_and(has_left, jnp.logical_or(both_near, jnp.logical_not(goes_first))))
        def _():
            ll_copy.start()

    pl.when(jnp.logical_not(left_is_far))(send_later)

    def all_steps(body):
        @pl.loop(0, ITERS * PAIRS)
        def _(n):
            t, g = n // PAIRS + 1, n % PAIRS
            body(t, g, [g * PAIR + k for k in range(PAIR)], n)

    last = ITERS * PAIRS - 1

    @pl.when(left_is_far)
    def _():
        @pl.loop(0, PAIRS)
        def _(g):
            heavy_part(1, g, False)

        @pl.when(jnp.logical_not(goes_first))
        def _():
            pl.delay(1500)

        send_later()
        late_far()

        @all_steps
        def _(t, g, chunks, n):
            pl.when(n == last)(finish_x)
            for h in chunks:
                ghost_part(t, h, held=True)
                end_part(t + 1, h, guarded=True)
            pl.when(t < ITERS)(lambda: heavy_part(t + 1, g, False))

    @pl.when(right_is_far)
    def _():
        @all_steps
        def _(t, g, chunks, n):
            for k, h in enumerate(chunks):
                ghost_part(t, h, sends_p=False)
                if k == 0:
                    pl.when(n == PAIRS)(late_far)
                end_part(t, h, sends_p=True)
            heavy_part(t, g, True)
            pl.when(n == last)(finish_x)

    @pl.when(both_near)
    def _():
        @all_steps
        def _(t, g, chunks, n):
            for k, h in enumerate(chunks):
                end_part(t, h)
                if k == PAIR - 1:
                    pl.when(n == last)(finish_x)
                ghost_part(t, h)
            heavy_part(t, g, True)
            pl.when(n == PAIRS - 1)(late_far)

    end = jnp.zeros((RHS, H), F32)
    for j in range(SLOTS):
        out_r[0, 0, j] = placed(r_in[:, j % 3].reshape(RHS, H), end, j)

    @pl.when(jnp.logical_and(jnp.logical_not(left_is_far), has_right))
    def _():
        @pl.loop(0, CHUNKS)
        def _(h):
            q_copy(ITERS, h).wait_recv()
            r_end[h] = r_end[h] - (p_out[ITERS, h] + far_out[h] + q_got[ITERS, h])

    end = jnp.transpose(r_end[...].reshape(RHS, H))
    for j in range(SLOTS):
        out_r[0, 0, j] = jnp.where(c - 1 == j, end, out_r[0, 0, j])

    @pl.when(has_left)
    def _():
        ll_copy.wait_send()
        for h in range(CHUNKS):
            q_copy(ITERS, h).wait_send()


def put_out(x, r, out_x, out_r, sems):
    stores = [pltpu.make_async_copy(x, out_x, sems.at[0]), pltpu.make_async_copy(r, out_r, sems.at[1])]
    for store in stores:
        store.start()
    for store in stores:
        store.wait()


def shards(far, operators, counts, pair_rows, gap):
    hbm = pl.BlockSpec(memory_space=pltpu.HBM)
    vmem = pl.BlockSpec(memory_space=pltpu.VMEM)
    dma = pltpu.SemaphoreType.DMA
    message = pltpu.VMEM((ITERS + 1, CHUNKS, W, H), F32)
    chunk = pltpu.VMEM((CHUNKS, W, H), F32)
    inner = pltpu.VMEM((CHUNKS, 3, W, H), F32)
    operator = pltpu.VMEM((2, H, H), BF16)
    block = jax.ShapeDtypeStruct((1, 1, SLOTS, H, RHS), F32)
    results = pl.pallas_call(
        functools.partial(kernel, far),
        out_shape=(block, block),
        in_specs=[pl.BlockSpec(memory_space=pltpu.SMEM), hbm, hbm, hbm],
        out_specs=(vmem, vmem),
        scratch_shapes=[
            pltpu.VMEM((SLOTS, M, M), F32),
            pltpu.VMEM((SLOTS, H, RHS), F32),
            pltpu.VMEM((SLOTS, H), jnp.int32),
            pltpu.VMEM((3, 2, 3 * H, H), BF16),
            pltpu.VMEM((2, 2 * H, H), BF16),
            operator,
            operator,
            operator,
            pltpu.VMEM((2, PAIR * W, 4 * H), BF16),
            chunk, chunk, chunk, chunk, chunk, chunk, chunk, chunk, chunk, chunk,
            inner, inner, inner,
            chunk,
            message, message, message, message,
            pltpu.VMEM((H, H), F32),
            pltpu.VMEM((H, H), F32),
            dma((SLOTS,)),
            dma((2,)),
            dma((2,)),
            dma((CHUNKS,)),
            dma((ITERS + 1, CHUNKS)),
            dma((CHUNKS,)),
            dma((ITERS + 1, CHUNKS)),
        ],
        compiler_params=pltpu.CompilerParams(
            collective_id=0, has_side_effects=True, vmem_limit_bytes=55_200_000),
        name="feti_chebyshev",
    )(counts, pltpu.with_memory_space_constraint(pair_rows, pltpu.HBM), operators, gap)
    return pl.pallas_call(
        put_out,
        out_shape=(block, block),
        in_specs=[vmem, vmem],
        out_specs=(hbm, hbm),
        scratch_shapes=[dma((2,))],
        compiler_params=pltpu.CompilerParams(vmem_limit_bytes=8 * 1024 * 1024),
        name="put_out",
    )(*results)


def solution(mesh):
    return jax.shard_map(
        functools.partial(shards, 16 if mesh.shape["sub"] % 16 == 0 else 2),
        mesh=mesh,
        in_specs=(
            P("grp", "sub", None, None, None),
            P("grp", "sub"),
            P("grp", "sub", None, None),
            P("grp", "sub", None, None, None),
        ),
        out_specs=(P("grp", "sub", None, None, None), P("grp", "sub", None, None, None)),
        check_vma=False,
    )
```
